32 devices in a mesh: groups: 2 (over y), frame: 8 (over z, x), row: 2 (over core).
Axes of the slice: x: 2, y: 2, z: 4, core: 2. Of those that a mesh axis runs over, the one named last changes fastest.
Arguments:
- latents: bfloat16 [16, 1024, 256], P(('groups', 'frame'), 'row'), parts along dimension 0, may hold values from -8 to 8
- ref_frames: int32 [16, 2], P(('groups', 'frame')), parts along dimension 0, may hold values from 0 to 7, as said below
- windows: int32 [16], P(('groups', 'frame')), parts along dimension 0, may hold values from 1 to 2, as said below
- quant_level: int32 [16], P(('groups', 'frame')), parts along dimension 0, may hold values from 0 to 63
- quant_scale: float32 [64, 256], replicated, may hold values from 0.5 to 2
- shared_proj: bfloat16 [256, 256], replicated, may hold values from -0.375 to 0.375
- value_proj: bfloat16 [256, 256], replicated, may hold values from -0.375 to 0.375
- output_proj: bfloat16 [256, 256], replicated, may hold values from -0.75 to 0.75
- conv_taps: bfloat16 [3, 256, 256], replicated, may hold values from -0.21875 to 0.21875
- cotangent: bfloat16 [16, 1024, 256], P(('groups', 'frame'), 'row'), parts along dimension 0, may hold values from -6 to 6
Outputs:
- coded_latent: bfloat16 [16, 1024, 256], P(('groups', 'frame'), 'row'), parts along dimension 0
- grad_latents: bfloat16 [16, 1024, 256], P(('groups', 'frame'), 'row'), parts along dimension 0
- grad_shared: float32 [512, 256], P('groups'), parts along dimension 0
- grad_values: float32 [512, 256], P('groups'), parts along dimension 0
- grad_output: float32 [512, 256], P('groups'), parts along dimension 0
- grad_taps: float32 [6, 256, 256], P('groups'), parts along dimension 0
The draws below stay inside these ranges and needn't reach their ends.
There are 2 independent parts, one for each index of `groups`. The reference program is written for one: setup_inputs(seed, part) draws one part's arguments, and reference() takes and returns one part's arrays. A program takes and returns all parts, laid end to end along the dimension named above; an argument that names none is the same for every part. Nothing has to cross between parts.
Inputs may be any that keep to these rules, and one draw needn't show every extreme that they name: ref_frames[f, s] differs from f by a power of two no larger than 2 ** 2, and that largest distance occurs. `windows`: some frame has a window of 2 rows.
All inputs are finite; a program needn't handle non-finite values.
Results may differ from the reference program's by a relative error of at most 0.0045.
The reference program's roundings to bfloat16 on the way count: a program that leaves them out, or rounds other values in their place, can miss the bound.
Values may be sent and summed in bfloat16 or wider, within the bound.
A program may use at most 128 MiB of HBM per device.

```python
import math
import jax
import jax.numpy as jnp
from jax import lax

C = 256
HEADS = 8
DH = 32
COLS = 64
QROWS = 8
WMAX = 2
LEVELS = 3
NQ = 64
FRAMES = 8
HROWS = 16
TOKF = 1024


def draw_latents(key, part):
    shape = (FRAMES, HROWS * COLS, C)
    values = jnp.clip(jax.random.normal(jax.random.fold_in(key, 1), shape, jnp.float32), -4.0, 4.0)
    return values.astype(jnp.bfloat16)


def draw_ref_frames(key, part):
    depth = jax.random.randint(jax.random.fold_in(key, 1), (FRAMES, 2), 0, LEVELS)
    depth = depth.at[0, 0].set(LEVELS - 1)
    distance = jnp.left_shift(jnp.ones((FRAMES, 2), jnp.int32), depth.astype(jnp.int32))
    side = jax.random.randint(jax.random.fold_in(key, 2), (FRAMES, 2), 0, 2)
    frame_ids = jnp.arange(FRAMES, dtype=jnp.int32)[:, None]
    earlier = frame_ids - distance
    later = frame_ids + distance
    pick_earlier = jnp.where(side == 0, earlier >= 0, later > FRAMES - 1)
    return jnp.where(pick_earlier, earlier, later).astype(jnp.int32)


def draw_windows(key, part):
    window = jax.random.randint(jax.random.fold_in(key, 3), (FRAMES,), 1, WMAX + 1)
    return window.at[0].set(WMAX).astype(jnp.int32)


def with_ends(drawn, stream_key, low, largest):
    shape = drawn.shape
    place = [jax.random.randint(jax.random.fold_in(stream_key, axis), (), 0, shape[axis]) for axis in range(len(shape))]
    drawn = drawn.at[tuple(place)].set(low)
    longest = shape.index(max(shape))
    place[longest] = (place[longest] + 1) % shape[longest]
    return drawn.at[tuple(place)].set(largest)


def shard_levels(key, extent, shards, low, largest):
    factor_of, own = 1.0, jax.random.fold_in(key, 6)
    for position, parts in shards:
        draws = jnp.exp(jax.random.uniform(jax.random.fold_in(own, position), (parts,), jnp.float32, low / len(shards), largest / len(shards)))
        factor_of = factor_of * jnp.repeat(draws, extent[position] // parts).reshape([-1 if axis == position else 1 for axis in range(len(extent))])
    return factor_of


def noise(rng, dims, scale, most, split=(), kind=jnp.bfloat16):
    loudness = shard_levels(rng, dims, split, -0.22, 0.18) if split else 1.0
    array = jax.random.normal(rng, dims, jnp.float32) * scale * loudness
    return jnp.minimum(jnp.maximum(array, -most), most).astype(kind)


def setup_inputs(seed: int = 0, part: int = 0) -> dict:
    seeds = jax.random.split(jax.random.key(seed), 11)
    own_keys = jax.random.split(jax.random.fold_in(seeds[10], part), 11)
    latents = draw_latents(jax.random.fold_in(jax.random.fold_in(seeds[10], part), 71), part)
    ref_frames = draw_ref_frames(jax.random.fold_in(jax.random.fold_in(seeds[10], part), 71), part)
    windows = draw_windows(jax.random.fold_in(jax.random.fold_in(seeds[10], part), 71), part)
    quant_level = with_ends(jax.random.randint(own_keys[3], (FRAMES,), 0, NQ), jax.random.fold_in(own_keys[3], 1), 0, NQ - 1).astype(jnp.int32)
    quant_scale = jnp.clip(jnp.exp(jax.random.uniform(seeds[4], (NQ, C), jnp.float32, math.log(0.5), math.log(2.0))), 0.5, 2.0)
    shared_proj = noise(seeds[5], (C, C), C ** -0.5, 0.375)
    value_proj = noise(seeds[6], (C, C), C ** -0.5, 0.375)
    output_proj = noise(seeds[7], (C, C), (C // 4) ** -0.5, 0.75)
    conv_taps = noise(seeds[8], (3, C, C), (3 * C) ** -0.5, 0.21875)
    cotangent = noise(own_keys[9], (FRAMES, TOKF, C), 1.0, 6.0, ((0, 8), (1, 2)))
    return {"latents": latents, "ref_frames": ref_frames, "windows": windows, "quant_level": quant_level, "quant_scale": quant_scale, "shared_proj": shared_proj, "value_proj": value_proj, "output_proj": output_proj, "conv_taps": conv_taps, "cotangent": cotangent}


SCORE_GAIN = 1.5
LAST_DIMS = (((1,), (1,)), ((), ()))
FIRST_DIMS = (((0,), (0,)), ((), ()))

def split_heads(block):
    return jnp.transpose(block.reshape(block.shape[0], HEADS, DH), (1, 0, 2))

def merge_heads(block):
    return jnp.transpose(block, (1, 0, 2)).reshape(block.shape[1], HEADS * DH)

def head_weights(query_head, key_head, allowed):
    scores = jnp.dot(query_head, key_head.T, preferred_element_type=jnp.float32) * (SCORE_GAIN / math.sqrt(DH))
    scores = jnp.where(allowed, scores, -jnp.inf)
    row_max = lax.optimization_barrier(jnp.max(scores, axis=1, keepdims=True))
    exp_terms = jnp.where(allowed, jnp.exp(scores - row_max), 0.0)
    return exp_terms / lax.optimization_barrier(jnp.sum(exp_terms, axis=1, keepdims=True))

def block_forward(query, keys, values, allowed):

    def one_head(head_parts):
        query_head, key_head, value_head = head_parts
        weights = head_weights(query_head, key_head, allowed)
        return jnp.dot(weights.astype(jnp.bfloat16), value_head, preferred_element_type=jnp.float32)
    result = lax.map(one_head, (split_heads(query), split_heads(keys), split_heads(values)))
    return merge_heads(result).astype(jnp.bfloat16)

def block_backward(query, keys, values, allowed, upstream):

    def one_head(head_parts):
        query_head, key_head, value_head, grad_head = head_parts
        weights = head_weights(query_head, key_head, allowed)
        prob = weights.astype(jnp.bfloat16)
        grad_prob = jnp.dot(grad_head, value_head.T, preferred_element_type=jnp.float32)
        value_grad = jnp.dot(prob.T, grad_head, preferred_element_type=jnp.float32)
        row_inner = lax.optimization_barrier(jnp.sum(weights * grad_prob, axis=1, keepdims=True))
        grad_score = (weights * (grad_prob - row_inner) * (SCORE_GAIN / math.sqrt(DH))).astype(jnp.bfloat16)
        query_grad = jnp.dot(grad_score, key_head, preferred_element_type=jnp.float32)
        key_grad = jnp.dot(grad_score.T, query_head, preferred_element_type=jnp.float32)
        return (query_grad, key_grad, value_grad)
    query_grad, key_grad, value_grad = lax.map(one_head, (split_heads(query), split_heads(keys), split_heads(values), split_heads(upstream)))
    return (merge_heads(query_grad), merge_heads(key_grad), merge_heads(value_grad))

def allowed_mask(begin_row, window, total_rows):
    key_span = QROWS + 2 * WMAX
    query_rows = begin_row + jnp.repeat(jnp.arange(QROWS, dtype=jnp.int32), COLS)
    key_rows = jnp.tile(jnp.repeat(begin_row - WMAX + jnp.arange(key_span, dtype=jnp.int32), COLS), 2)
    nearby = jnp.abs(query_rows[:, None] - key_rows[None, :]) <= window
    inside = (key_rows >= 0) & (key_rows < total_rows)
    return nearby & inside[None, :]

def add_window(summed, addend, begin_row):
    current = lax.dynamic_slice_in_dim(summed, begin_row, addend.shape[1], 1)
    return lax.dynamic_update_slice_in_dim(summed, current + addend, begin_row, 1)

def against(left_side, weight):
    return lax.dot_general(left_side, weight, LAST_DIMS, preferred_element_type=jnp.float32)

def cross_rows(left_side, right_side):
    return lax.dot_general(left_side, right_side, FIRST_DIMS, preferred_element_type=jnp.float32)

def exact_against(left_side, weight):
    return lax.dot_general(left_side, weight.astype(jnp.float32), LAST_DIMS, precision=lax.Precision.HIGHEST, preferred_element_type=jnp.float32)

def exact_cross(left_side, right_side):
    return lax.dot_general(left_side.astype(jnp.float32), right_side, FIRST_DIMS, precision=lax.Precision.HIGHEST, preferred_element_type=jnp.float32)

def reference(latents, ref_frames, windows, quant_level, quant_scale, shared_proj, value_proj, output_proj, conv_taps, cotangent):
    frames = latents.shape[0]
    width = latents.shape[2]
    flat_rows = latents.reshape(-1, width)
    queries = jnp.dot(flat_rows, shared_proj, preferred_element_type=jnp.float32).astype(jnp.bfloat16)
    value_rows = jnp.dot(flat_rows, value_proj, preferred_element_type=jnp.float32).astype(jnp.bfloat16)
    query_grid = queries.reshape(frames, HROWS, COLS, width)
    value_grid = value_rows.reshape(frames, HROWS, COLS, width)
    margins = ((0, 0), (WMAX, WMAX), (0, 0), (0, 0))
    query_pad = jnp.pad(query_grid, margins)
    value_pad = jnp.pad(value_grid, margins)
    key_span = QROWS + 2 * WMAX
    ext_rows = HROWS + 2 * WMAX
    block_ids = jnp.arange(HROWS // QROWS, dtype=jnp.int32)

    def gather_slots(frame):
        ref_pair = ref_frames[frame]
        keys = jnp.stack([query_pad[ref_pair[0]], query_pad[ref_pair[1]]])
        values = jnp.stack([value_pad[ref_pair[0]], value_pad[ref_pair[1]]])
        return (keys, values)

    def block_parts(frame, keys, values, block):
        begin_row = block * QROWS
        query = lax.dynamic_slice_in_dim(query_grid[frame], begin_row, QROWS, 0).reshape(-1, width)
        key_block = lax.dynamic_slice_in_dim(keys, begin_row, key_span, 1).reshape(-1, width)
        value_block = lax.dynamic_slice_in_dim(values, begin_row, key_span, 1).reshape(-1, width)
        allowed = allowed_mask(begin_row, windows[frame], HROWS)
        return (query, key_block, value_block, allowed)

    def frame_forward(frame):
        keys, values = gather_slots(frame)

        def one_block(block):
            query, key_block, value_block, allowed = block_parts(frame, keys, values, block)
            return block_forward(query, key_block, value_block, allowed)
        return lax.map(one_block, block_ids).reshape(HROWS * COLS, width)
    mixed_rows = lax.map(frame_forward, jnp.arange(frames, dtype=jnp.int32)).reshape(-1, width)
    residual = flat_rows.astype(jnp.float32) + jnp.dot(mixed_rows, output_proj, preferred_element_type=jnp.float32)
    hidden = residual.astype(jnp.bfloat16).reshape(frames, HROWS, COLS, width)
    hidden_pad = jnp.pad(hidden, ((0, 0), (1, 1), (0, 0), (0, 0)))
    context = jnp.zeros_like(residual)
    for tap_shift in (-1, 0, 1):
        shifted = hidden_pad[:, 1 + tap_shift:1 + tap_shift + HROWS].reshape(-1, width)
        context = context + jnp.dot(shifted, conv_taps[tap_shift + 1], preferred_element_type=jnp.float32)
    gain_rows = quant_scale[quant_level]
    coded_latent = ((residual + context).reshape(frames, -1, width) * gain_rows[:, None, :]).astype(jnp.bfloat16)
    grad_z = cotangent.astype(jnp.float32) * gain_rows[:, None, :]
    grad_zb = grad_z.astype(jnp.bfloat16)
    grad_pad = jnp.pad(grad_zb.reshape(frames, HROWS, COLS, width), ((0, 0), (1, 1), (0, 0), (0, 0)))
    grad_resid = grad_z.reshape(-1, width)
    for tap_shift in (-1, 0, 1):
        shifted = grad_pad[:, 1 - tap_shift:1 - tap_shift + HROWS].reshape(-1, width)
        grad_resid = grad_resid + against(shifted, conv_taps[tap_shift + 1])
    grad_rb = grad_resid.astype(jnp.bfloat16)
    grad_mixed = against(grad_rb, output_proj).astype(jnp.bfloat16).reshape(frames, HROWS, COLS, width)
    zero_sums = jnp.zeros((frames, ext_rows, COLS, width), jnp.float32)

    def frame_backward(running, frame):
        key_sums, value_sums = running
        keys, values = gather_slots(frame)

        def one_block(inner_sums, block):
            query_grad, key_grad, value_grad = inner_sums
            query, key_block, value_block, allowed = block_parts(frame, keys, values, block)
            begin_row = block * QROWS
            upstream = lax.dynamic_slice_in_dim(grad_mixed[frame], begin_row, QROWS, 0).reshape(-1, width)
            block_query, block_key, block_value = block_backward(query, key_block, value_block, allowed, upstream)
            query_grad = lax.dynamic_update_slice_in_dim(query_grad, block_query.reshape(QROWS, COLS, width), begin_row, 0)
            key_grad = add_window(key_grad, block_key.reshape(2, key_span, COLS, width), begin_row)
            value_grad = add_window(value_grad, block_value.reshape(2, key_span, COLS, width), begin_row)
            return ((query_grad, key_grad, value_grad), None)
        initial = (jnp.zeros((HROWS, COLS, width), jnp.float32), jnp.zeros((2, ext_rows, COLS, width), jnp.float32), jnp.zeros((2, ext_rows, COLS, width), jnp.float32))
        (query_grad, key_grad, value_grad), _ = lax.scan(one_block, initial, block_ids)
        ref_pair = ref_frames[frame]
        key_sums = key_sums.at[ref_pair[0]].add(key_grad[0]).at[ref_pair[1]].add(key_grad[1])
        value_sums = value_sums.at[ref_pair[0]].add(value_grad[0]).at[ref_pair[1]].add(value_grad[1])
        return ((key_sums, value_sums), query_grad)
    (key_sums, value_sums), query_grads = lax.scan(frame_backward, (zero_sums, zero_sums), jnp.arange(frames, dtype=jnp.int32))
    grad_proj = (query_grads + key_sums[:, WMAX:WMAX + HROWS]).reshape(-1, width)
    grad_vals = value_sums[:, WMAX:WMAX + HROWS].reshape(-1, width)
    grad_latents = grad_resid + exact_against(grad_proj, shared_proj) + exact_against(grad_vals, value_proj)
    grad_latents = grad_latents.astype(jnp.bfloat16).reshape(frames, -1, width)
    norm_scale = 1.0 / math.sqrt(frames * HROWS * COLS)
    grad_shared = exact_cross(flat_rows, grad_proj) * norm_scale
    grad_values = exact_cross(flat_rows, grad_vals) * norm_scale
    grad_output = cross_rows(mixed_rows, grad_rb) * norm_scale
    flat_grad = grad_zb.reshape(-1, width)
    grad_taps = jnp.stack([cross_rows(hidden_pad[:, 1 + tap_shift:1 + tap_shift + HROWS].reshape(-1, width), flat_grad) for tap_shift in (-1, 0, 1)]) * norm_scale
    return (coded_latent, grad_latents, grad_shared, grad_values, grad_output, grad_taps)
```

```python
import functools
import math

import jax
import jax.numpy as jnp
from jax import lax
from jax.experimental import pallas as pl
from jax.experimental.pallas import tpu as pltpu
from jax.sharding import PartitionSpec as P

HEADS = 8
DH = 32
COLS = 64
WMAX = 2

SCORE_SCALE = 1.5 / math.sqrt(DH)
LOG2E = math.log2(math.e)
BF = jnp.bfloat16
F32 = jnp.float32


def mm(a, b, ca=1, cb=0):
    return lax.dot_general(a, b, (((ca,), (cb,)), ((), ())), preferred_element_type=F32)


HALF = 4


def masked_rows(block, f0):
    lane = lax.broadcasted_iota(jnp.int32, (1, HALF * DH), 1) // DH
    part = block[:, f0 : f0 + HALF * DH]
    return jnp.concatenate(
        [jnp.where(lane == h, part, jnp.zeros_like(part)) for h in range(HALF)], axis=0
    )


def head_diagonal(wide):
    rows = wide.T
    lane = lax.broadcasted_iota(jnp.int32, (1, HALF * DH), 1) // DH
    out = rows[:COLS]
    for h in range(1, HALF):
        out = jnp.where(lane == h, rows[h * COLS : (h + 1) * COLS], out)
    return out


def forward_row(i, bias, k_ref, qm_ref, p_ref, pb_ref, inv_ref):
    band = 2 * COLS
    reach = 2 * WMAX + 1
    wide = HALF * COLS
    base = i * band
    kk = SCORE_SCALE * LOG2E
    for hf in range(2):
        f0 = hf * HALF * DH
        ft = slice(f0, f0 + HALF * DH)
        p_ref[i, hf] = mm(k_ref[base : base + reach * band, ft], qm_ref[i, hf], 1, 1)
        m8 = None
        for c in range(reach):
            x = p_ref[i, hf, c * band : (c + 1) * band, :].reshape(band // 8, 8, wide)
            top = jnp.max(x, axis=0) + bias[c]
            m8 = top if m8 is None else jnp.maximum(m8, top)
        m = jnp.max(m8, axis=0, keepdims=True)
        l8 = jnp.zeros((8, wide), F32)
        for c in range(reach):
            sl = slice(c * band, (c + 1) * band)
            p = jnp.exp2(p_ref[i, hf, sl, :] * kk + (bias[c] - m) * kk)
            p_ref[i, hf, sl, :] = p
            l8 = l8 + jnp.sum(p.reshape(band // 8, 8, wide), axis=0)
        inv = 1.0 / jnp.sum(l8, axis=0, keepdims=True)
        inv_ref[i, hf] = inv
        for c in range(reach):
            sl = slice(c * band, (c + 1) * band)
            pb_ref[i, hf, sl, :] = (p_ref[i, hf, sl, :] * inv).astype(BF)


def mix_row(i, vt_ref, pb_ref, mix_ref):
    band = 2 * COLS
    reach = 2 * WMAX + 1
    base = i * band
    for hf in range(2):
        f0 = hf * HALF * DH
        ft = slice(f0, f0 + HALF * DH)
        mix = mm(vt_ref[ft, base : base + reach * band], pb_ref[i, hf])
        mix_ref[i * COLS : (i + 1) * COLS, ft] = head_diagonal(mix).astype(BF)


def score_row(i, v_ref, dom_ref, p_ref, inv_ref, dp_ref, ds_ref):
    band = 2 * COLS
    reach = 2 * WMAX + 1
    wide = HALF * COLS
    base = i * band
    win = slice(base, base + reach * band)
    for hf in range(2):
        f0 = hf * HALF * DH
        ft = slice(f0, f0 + HALF * DH)
        dp_ref[i, hf] = mm(v_ref[win, ft], dom_ref[i, hf], 1, 1)
        u8 = jnp.zeros((8, wide), F32)
        for c in range(reach):
            sl = slice(c * band, (c + 1) * band)
            x = p_ref[i, hf, sl, :] * dp_ref[i, hf, sl, :]
            u8 = u8 + jnp.sum(x.reshape(band // 8, 8, wide), axis=0)
        inv = inv_ref[i, hf]
        ci = inv * SCORE_SCALE
        inner = jnp.sum(u8, axis=0, keepdims=True) * inv * ci
        for c in range(reach):
            sl = slice(c * band, (c + 1) * band)
            ds_ref[i, hf, sl, :] = (p_ref[i, hf, sl, :] * (dp_ref[i, hf, sl, :] * ci - inner)).astype(BF)


def query_row(i, kt_ref, ds_ref, dq_ref):
    band = 2 * COLS
    base = i * band
    win = slice(base, base + (2 * WMAX + 1) * band)
    for hf in range(2):
        f0 = hf * HALF * DH
        ft = slice(f0, f0 + HALF * DH)
        dq = mm(kt_ref[ft, win], ds_ref[i, hf])
        dq_ref[i * COLS : (i + 1) * COLS, ft] = head_diagonal(dq).astype(BF)


def key_row(i, qm_ref, dom_ref, pb_ref, ds_ref, dk_ref, dv_ref):
    band = 2 * COLS
    base = i * band
    win = slice(base, base + (2 * WMAX + 1) * band)
    for hf in range(2):
        f0 = hf * HALF * DH
        ft = slice(f0, f0 + HALF * DH)
        dk_ref[win, ft] += mm(ds_ref[i, hf], qm_ref[i, hf])
        dv_ref[win, ft] += mm(pb_ref[i, hf], dom_ref[i, hf])


def attention_kernel(
    meta_ref, buf_hbm, halo_hbm, x_hbm, q_hbm, do_hbm, resid_hbm,
    sp_ref, vp_ref, op_ref,
    residual_ref, hidden_ref, base_ref, part_ref, gs_ref, gv_ref, go_ref,
    xs_ref, xi_ref, k_ref, v_ref, kt_ref, vt_ref, mix_ref, dq_ref, dk_ref, dv_ref,
    p_ref, pb_ref, inv_ref, dp_ref, ds_ref, qm_ref, dom_ref,
    x_ref, q_ref, do_ref, resid_ref, sems,
):
    tokens, width = q_ref.shape
    rows = tokens // COLS
    rim = WMAX * COLS
    window = meta_ref[2]
    row_id = meta_ref[3]
    first_row = row_id * rows
    total_rows = meta_ref[4]
    bottom = rim + tokens
    held = pl.multiple_of(jnp.where(row_id == 0, bottom, 0), rim)
    empty = pl.multiple_of(jnp.where(row_id == 0, 0, bottom), rim)
    moves = [(q_hbm, q_ref), (do_hbm, do_ref)]
    for s in range(2):
        kind = meta_ref[s]
        moves.append((buf_hbm.at[kind], xs_ref.at[s, pl.ds(rim, tokens)]))
        moves.append((halo_hbm.at[kind], xs_ref.at[s, pl.ds(held, rim)]))
    moves += [(x_hbm, x_ref), (resid_hbm, resid_ref)]
    copies = [
        pltpu.make_async_copy(source, target, sems.at[i])
        for i, (source, target) in enumerate(moves)
    ]
    for move in copies:
        move.start()
    dk_ref[...] = jnp.zeros_like(dk_ref)
    dv_ref[...] = jnp.zeros_like(dv_ref)
    copies[0].wait()
    copies[1].wait()
    for i in range(rows):
        tok = slice(i * COLS, (i + 1) * COLS)
        for hf in range(2):
            qm_ref[i, hf] = masked_rows(q_ref[tok, :], hf * HALF * DH)
            dom_ref[i, hf] = masked_rows(do_ref[tok, :], hf * HALF * DH)
    for s in range(2):
        xs_ref[s, pl.ds(empty, rim), :] = jnp.zeros((rim, width), BF)
        copies[2 * s + 2].wait()
        copies[2 * s + 3].wait()
        for e in range(rows + 2 * WMAX):
            xi_ref[(2 * e + s) * COLS : (2 * e + s + 1) * COLS, :] = xs_ref[
                s, e * COLS : (e + 1) * COLS, :
            ]
    xi = xi_ref[...]
    keys = mm(xi, sp_ref[...]).astype(BF)
    k_ref[...] = keys
    kt_ref[...] = keys.T
    vals = mm(xi, vp_ref[...]).astype(BF)
    v_ref[...] = vals
    vt_ref[...] = vals.T

    def bias_of(i):
        out = []
        for c in range(2 * WMAX + 1):
            key_row = first_row + i + c - WMAX
            inside = (key_row >= 0) & (key_row < total_rows) & (abs(c - WMAX) <= window)
            out.append(jnp.where(inside, 0.0, -jnp.inf).astype(F32))
        return out

    for i in range(rows):
        forward_row(i, bias_of(i), k_ref, qm_ref, p_ref, pb_ref, inv_ref)
    for i in range(rows):
        mix_row(i, vt_ref, pb_ref, mix_ref)
    for i in range(rows + 1):
        if i < rows:
            score_row(i, v_ref, dom_ref, p_ref, inv_ref, dp_ref, ds_ref)
        if i:
            key_row(i - 1, qm_ref, dom_ref, pb_ref, ds_ref, dk_ref, dv_ref)
            query_row(i - 1, kt_ref, ds_ref, dq_ref)
    for move in copies[6:]:
        move.wait()

    dq = dq_ref[...]
    base_ref[...] = resid_ref[...] + mm(dq, sp_ref[...], 1, 1)
    mix = mix_ref[...]
    go_ref[...] = mm(mix.T, resid_ref[...].astype(BF))
    residual = x_ref[...].astype(F32) + mm(mix, op_ref[...])
    residual_ref[...] = residual
    hidden_ref[...] = residual.astype(BF)
    dk = dk_ref[...].astype(BF)
    dv = dv_ref[...].astype(BF)
    part = mm(dk, sp_ref[...], 1, 1) + mm(dv, vp_ref[...], 1, 1)
    for e in range(rows + 2 * WMAX):
        for s in range(2):
            part_ref[s, e * COLS : (e + 1) * COLS, :] = part[
                (2 * e + s) * COLS : (2 * e + s + 1) * COLS, :
            ]
    xit = xi_ref[...].T
    gs_ref[...] = mm(x_ref[...].T, dq) + mm(xit, dk)
    gv_ref[...] = mm(xit, dv)


def attention(meta, buf, halo, x, q, do, resid, shared, value, output):
    tokens, width = q.shape
    rows = tokens // COLS
    ext = tokens + 2 * WMAX * COLS
    keys = 2 * (2 * WMAX + 1) * COLS
    wide = HALF * COLS
    vm = pl.BlockSpec(memory_space=pltpu.VMEM)
    full = jax.ShapeDtypeStruct((tokens, width), F32)
    square = jax.ShapeDtypeStruct((width, width), F32)
    return pl.pallas_call(
        attention_kernel,
        out_shape=(
            full,
            jax.ShapeDtypeStruct((tokens, width), BF),
            full,
            jax.ShapeDtypeStruct((2, ext, width), F32),
            square, square, square,
        ),
        in_specs=[pl.BlockSpec(memory_space=pltpu.SMEM)]
        + [pl.BlockSpec(memory_space=pltpu.MemorySpace.HBM)] * 6
        + [vm] * 3,
        out_specs=(vm,) * 7,
        scratch_shapes=[
            pltpu.VMEM((2, ext, width), BF),
            pltpu.VMEM((2 * ext, width), BF),
            pltpu.VMEM((2 * ext, width), BF),
            pltpu.VMEM((2 * ext, width), BF),
            pltpu.VMEM((width, 2 * ext), BF),
            pltpu.VMEM((width, 2 * ext), BF),
            pltpu.VMEM((tokens, width), BF),
            pltpu.VMEM((tokens, width), BF),
            pltpu.VMEM((2 * ext, width), F32),
            pltpu.VMEM((2 * ext, width), F32),
            pltpu.VMEM((rows, 2, keys, wide), F32),
            pltpu.VMEM((rows, 2, keys, wide), BF),
            pltpu.VMEM((rows, 2, 1, wide), F32),
            pltpu.VMEM((rows, 2, keys, wide), F32),
            pltpu.VMEM((rows, 2, keys, wide), BF),
            pltpu.VMEM((rows, 2, wide, HALF * DH), BF),
            pltpu.VMEM((rows, 2, wide, HALF * DH), BF),
            pltpu.VMEM((tokens, width), BF),
            pltpu.VMEM((tokens, width), BF),
            pltpu.VMEM((tokens, width), BF),
            pltpu.VMEM((tokens, width), F32),
            pltpu.SemaphoreType.DMA((8,)),
        ],
        compiler_params=pltpu.CompilerParams(vmem_limit_bytes=64_000_000),
        cost_estimate=pl.CostEstimate(
            flops=int(2e10), bytes_accessed=int(8e6), transcendentals=int(4e6)
        ),
        name="attention",
    )(meta, buf, halo, x, q, do, resid, shared, value, output)


MESH = pl.DeviceIdType.MESH
CHUNKS = 4


def greet(targets):
    barrier = pltpu.get_barrier_semaphore()
    count = 0
    for exists, device in targets:

        @pl.when(exists)
        def _(device=device):
            pl.semaphore_signal(barrier, inc=1, device_id=device, device_id_type=MESH)

        count = count + jnp.where(exists, 1, 0)
    pl.semaphore_wait(barrier, count)


def fetch_kernel(
    frames, level_ref, x_ref, ct_ref, qs_ref, sp_ref, op_ref, taps_ref,
    buf_ref, halo_ref, q_ref, do_ref, gzb_ref, resid_ref, gain_ref,
    cth_ref, ext_ref, ssem, rsem, hs, hr, cs, cr,
):
    f = lax.axis_index("frame")
    r = lax.axis_index("row")
    tokens = x_ref.shape[0]
    odd = lax.rem(f, 2)
    pair = f + 1 - 2 * odd
    lo2, hi2, lo4, hi4 = f >= 2, f + 2 < frames, f >= 4, f + 4 < frames
    side = ((odd == 1) & (f + 1 < frames)) | ((odd == 0) & (f >= 1))
    always = f >= 0
    have = (lo2, hi2, always, lo4, hi4, side)
    partner = {"row": 1 - r}
    up, down, across = {"frame": f + 2}, {"frame": f - 2}, {"frame": pair}
    greet(((hi2, up), (lo2, down), (always, across), (always, partner)))

    edge = ct_ref.shape[0] - COLS
    ct_copy = pltpu.make_async_remote_copy(
        ct_ref.at[pl.ds(pl.multiple_of((1 - r) * edge, COLS), COLS)], cth_ref, cs, cr,
        device_id=partner, device_id_type=MESH,
    )
    ct_copy.start()
    step = tokens // CHUNKS

    def copy(kind, c, source, device):
        part = pl.ds(c * step, step)
        return pltpu.make_async_remote_copy(
            source.at[part], buf_ref.at[kind, part], ssem.at[kind, c], rsem.at[kind, c],
            device_id=device, device_id_type=MESH,
        )

    for c in range(CHUNKS):

        @pl.when(hi2)
        def _():
            copy(0, c, x_ref, up).start()

        @pl.when(lo2)
        def _():
            copy(1, c, x_ref, down).start()

        copy(2, c, x_ref, across).start()

    for c in range(CHUNKS):

        @pl.when(lo2)
        def _():
            copy(0, c, x_ref, across).wait_recv()

        @pl.when(lo2 & hi2)
        def _():
            copy(3, c, buf_ref.at[0], up).start()

        @pl.when(lo2 & (odd == 1))
        def _():
            copy(5, c, buf_ref.at[0], across).start()

        @pl.when(hi2)
        def _():
            copy(1, c, x_ref, across).wait_recv()

        @pl.when(hi2 & lo2)
        def _():
            copy(4, c, buf_ref.at[1], down).start()

        @pl.when(hi2 & (odd == 0))
        def _():
            copy(5, c, buf_ref.at[1], across).start()

    level = lax.broadcasted_iota(jnp.int32, (qs_ref.shape[0], 1), 0)
    gain = jnp.sum(
        jnp.where(level == level_ref[0], qs_ref[...], 0.0), axis=0, keepdims=True
    )
    gain_ref[...] = gain
    queries = mm(x_ref[...], sp_ref[...]).astype(BF)
    q_ref[...] = queries
    grad_z = ct_ref[...].astype(F32) * gain
    grad_zb = grad_z.astype(BF)
    gzb_ref[...] = grad_zb
    ct_copy.wait()
    outer = (cth_ref[...].astype(F32) * gain).astype(BF)
    blank = jnp.zeros_like(outer)
    ext_ref[COLS : COLS + tokens, :] = grad_zb

    @pl.when(r == 0)
    def _():
        ext_ref[:COLS, :] = blank
        ext_ref[COLS + tokens :, :] = outer

    @pl.when(r != 0)
    def _():
        ext_ref[:COLS, :] = outer
        ext_ref[COLS + tokens :, :] = blank

    resid = grad_z
    for t in range(3):
        resid = resid + mm(ext_ref[(2 - t) * COLS : (2 - t) * COLS + tokens, :], taps_ref[t], 1, 1)
    resid_ref[...] = resid
    grad_mixed = mm(resid.astype(BF), op_ref[...], 1, 1).astype(BF)
    do_ref[...] = grad_mixed

    rim = WMAX * COLS
    start = pl.multiple_of((1 - r) * (tokens - rim), rim)

    def halo(kind):
        return pltpu.make_async_remote_copy(
            buf_ref.at[kind, pl.ds(start, rim)], halo_ref.at[kind], hs.at[kind], hr.at[kind],
            device_id=partner, device_id_type=MESH,
        )

    for kind in range(6):

        @pl.when(have[kind])
        def _():
            if kind > 1:
                for c in range(CHUNKS):
                    copy(kind, c, x_ref, across).wait_recv()
            halo(kind).start()

    sent = (hi2, lo2, always, lo2 & hi2, lo2 & hi2, (lo2 & (odd == 1)) | (hi2 & (odd == 0)))
    for kind in range(6):

        @pl.when(have[kind])
        def _():
            halo(kind).wait()

        @pl.when(sent[kind])
        def _():
            for c in range(CHUNKS):
                copy(kind, c, x_ref, across).wait_send()


def fetch(level, tokens, cotangent, scale, shared, output, taps, frames):
    count, width = tokens.shape
    vm = pl.BlockSpec(memory_space=pltpu.VMEM)
    dma = pltpu.SemaphoreType.DMA
    rows = jax.ShapeDtypeStruct((count, width), BF)
    return pl.pallas_call(
        functools.partial(fetch_kernel, frames),
        out_shape=(
            jax.ShapeDtypeStruct((6, count, width), BF),
            jax.ShapeDtypeStruct((6, WMAX * COLS, width), BF),
            rows, rows, rows,
            jax.ShapeDtypeStruct((count, width), F32),
            jax.ShapeDtypeStruct((1, width), F32),
        ),
        in_specs=[pl.BlockSpec(memory_space=pltpu.SMEM)] + [vm] * 6,
        out_specs=(vm,) * 7,
        scratch_shapes=[
            pltpu.VMEM((COLS, width), BF),
            pltpu.VMEM((count + 2 * COLS, width), BF),
            dma((6, CHUNKS)), dma((6, CHUNKS)), dma((6,)), dma((6,)), dma(()), dma(()),
        ],
        compiler_params=pltpu.CompilerParams(collective_id=0, has_side_effects=True),
        name="fetch",
    )(level, tokens, cotangent, scale, shared, output, taps)


def reduce_kernel(
    frames, out_ref, base_ref, w_ref, lat_ref, wsum_ref,
    rb, sb, wp, ws, wr, ssem, rsem, ps, pr, rs_s, rs_r, ag_s, ag_r, fw_s, fw_r,
):
    f = lax.axis_index("frame")
    r = lax.axis_index("row")
    tokens = base_ref.shape[0]
    odd = lax.rem(f, 2)
    pair = f + 1 - 2 * odd
    lo2, hi2, lo4, hi4 = f >= 2, f + 2 < frames, f >= 4, f + 4 < frames
    always = f >= 0
    side = ((odd == 1) & (f + 1 < frames)) | ((odd == 0) & (f >= 1))
    relay = ((odd == 1) & lo2) | ((odd == 0) & hi2)
    partner = {"row": 1 - r}
    up, down, across = {"frame": f + 2}, {"frame": f - 2}, {"frame": pair}

    barrier = pltpu.get_barrier_semaphore()
    pl.semaphore_signal(barrier, inc=1, device_id=partner, device_id_type=MESH)

    def hello(k, carry):
        pl.semaphore_signal(
            barrier, inc=1, device_id={"frame": lax.rem(f + k, frames)}, device_id_type=MESH
        )
        return carry

    lax.fori_loop(1, frames, hello, 0)
    pl.semaphore_wait(barrier, frames)

    step = tokens // CHUNKS
    sent = (hi2, lo2, always, hi4, lo4, side)
    got = (lo2, hi2, always, lo2 & hi2, lo2 & hi2, relay)
    device = (up, down, across, up, down, across)

    def copy(kind, c, source):
        part = pl.ds(c * step, step)
        return pltpu.make_async_remote_copy(
            source.at[part], rb.at[kind, part], ssem.at[kind, c], rsem.at[kind, c],
            device_id=device[kind], device_id_type=MESH,
        )

    halves = pltpu.make_async_remote_copy(
        w_ref.at[1 - r], wp, ps, pr, device_id=partner, device_id_type=MESH
    )
    halves.start()
    for c in range(CHUNKS):
        for kind in (3, 4, 5):

            @pl.when(sent[kind])
            def _():
                copy(kind, c, out_ref.at[kind]).start()

    for kind in (0, 1, 3, 4, 5):

        @pl.when(jnp.logical_not(got[kind]))
        def _():
            rb[kind, :, :] = jnp.zeros((tokens, rb.shape[2]), BF)

    halves.wait()
    ws[...] = (w_ref[r] + wp[...]).astype(BF)

    def piece(ref, mine, other, target, s_sem, r_sem, slot, k):
        return pltpu.make_async_remote_copy(
            mine, other, s_sem.at[k], r_sem.at[slot],
            device_id={"frame": target}, device_id_type=MESH,
        )

    def scatter(k):
        target = lax.rem(f + k, frames)
        return piece(ws, ws.at[target], wr.at[f], target, rs_s, rs_r, f, k)

    def arrived(k):
        source = lax.rem(f - k + frames, frames)
        return source, piece(ws, ws.at[source], wr.at[source], source, rs_s, rs_r, source, k)

    def gather(k):
        target = lax.rem(f + k, frames)
        return piece(ws, wsum_ref.at[r, f], wsum_ref.at[r, f], target, ag_s, ag_r, f, k)

    def gathered(k):
        source = lax.rem(f - k + frames, frames)
        return source, piece(
            ws, wsum_ref.at[r, source], wsum_ref.at[r, source], source, ag_s, ag_r, source, k
        )

    def forward(j, own):
        return pltpu.make_async_remote_copy(
            wsum_ref.at[own, j], wsum_ref.at[own, j], fw_s.at[j], fw_r.at[j],
            device_id=partner, device_id_type=MESH,
        )

    def run(body):
        lax.fori_loop(1, frames, lambda k, carry: (body(k), carry)[1], 0)

    run(lambda k: scatter(k).start())
    for c in range(CHUNKS):
        copy(2, c, out_ref.at[2]).start()

    even = jnp.where(odd == 0, 1.0, 0.0).astype(F32)
    for c in range(CHUNKS):
        part = slice(c * step, (c + 1) * step)
        for kind in (3, 4, 5):

            @pl.when(got[kind])
            def _():
                copy(kind, c, out_ref.at[kind]).wait_recv()

        extra = rb[5, part, :].astype(F32)
        rising = out_ref[0, part, :].astype(F32) + rb[3, part, :].astype(F32) + extra * even
        falling = (
            out_ref[1, part, :].astype(F32) + rb[4, part, :].astype(F32) + extra * (1.0 - even)
        )
        sb[0, part, :] = rising.astype(BF)
        sb[1, part, :] = falling.astype(BF)

        @pl.when(hi2)
        def _():
            copy(0, c, sb.at[0]).start()

        @pl.when(lo2)
        def _():
            copy(1, c, sb.at[1]).start()

    def add_piece(k, total):
        source, waiting = arrived(k)
        waiting.wait_recv()
        return total + wr[source].astype(F32)

    total = lax.fori_loop(1, frames, add_piece, w_ref[r, f] + wp[f])
    wsum_ref[r, f] = total.astype(BF)
    run(lambda k: gather(k).start())
    forward(f, r).start()

    for c in range(CHUNKS):
        part = slice(c * step, (c + 1) * step)
        for kind in (0, 1, 2):

            @pl.when(got[kind])
            def _():
                copy(kind, c, out_ref.at[kind]).wait_recv()

        lat_ref[part, :] = (
            base_ref[part, :]
            + rb[0, part, :].astype(F32)
            + rb[1, part, :].astype(F32)
            + rb[2, part, :].astype(F32)
        ).astype(BF)

    def pass_on(k):
        source, waiting = gathered(k)
        waiting.wait_recv()
        forward(source, r).start()

    run(pass_on)

    def finish(k):
        scatter(k).wait_send()
        gather(k).wait_send()

    run(finish)

    def last(j, carry):
        forward(j, r).wait_send()
        forward(j, 1 - r).wait_recv()
        return carry

    lax.fori_loop(0, frames, last, 0)
    for kind in range(6):

        @pl.when(sent[kind])
        def _():
            for c in range(CHUNKS):
                copy(kind, c, out_ref.at[kind]).wait_send()


def reduce(outgoing, base, grads, frames):
    count, width = base.shape
    vm = pl.BlockSpec(memory_space=pltpu.VMEM)
    dma = pltpu.SemaphoreType.DMA
    pieces = grads.shape[1:]
    return pl.pallas_call(
        functools.partial(reduce_kernel, frames),
        out_shape=(
            jax.ShapeDtypeStruct((count, width), BF),
            jax.ShapeDtypeStruct(grads.shape, BF),
        ),
        in_specs=[vm] * 3,
        out_specs=(vm,) * 2,
        scratch_shapes=[
            pltpu.VMEM((6, count, width), BF),
            pltpu.VMEM((2, count, width), BF),
            pltpu.VMEM(pieces, F32),
            pltpu.VMEM(pieces, BF),
            pltpu.VMEM(pieces, BF),
            dma((6, CHUNKS)), dma((6, CHUNKS)), dma(()), dma(()),
            dma((frames,)), dma((frames,)), dma((frames,)), dma((frames,)),
            dma((frames,)), dma((frames,)),
        ],
        compiler_params=pltpu.CompilerParams(collective_id=1, has_side_effects=True),
        name="reduce",
    )(outgoing, base, grads)


def from_partner(value):
    return lax.ppermute(value, "row", [(0, 1), (1, 0)])


def row_halo(array, row_id, width):
    length = array.shape[-3]
    first = lax.slice_in_dim(array, 0, width, axis=array.ndim - 3)
    last = lax.slice_in_dim(array, length - width, length, axis=array.ndim - 3)
    got = from_partner(jnp.where(row_id == 0, last, first))
    zero = jnp.zeros_like(got)
    before = jnp.where(row_id == 0, zero, got)
    after = jnp.where(row_id == 0, got, zero)
    return jnp.concatenate([before, array, after], axis=array.ndim - 3)


def local(
    latents, ref_frames, windows, quant_level, quant_scale,
    shared_proj, value_proj, output_proj, conv_taps, cotangent,
):
    width = latents.shape[2]
    rows_dev = latents.shape[1] // COLS
    row_devs = lax.axis_size("row")
    total_rows = rows_dev * row_devs
    frame_id = lax.axis_index("frame")
    row_id = lax.axis_index("row")
    own_refs = ref_frames[0]
    ext_rows = rows_dev + 2 * WMAX
    grid = (rows_dev, COLS, width)
    tokens = latents[0]
    frames = lax.axis_size("frame")
    odd = frame_id % 2
    sources = (
        frame_id - 2, frame_id + 2, frame_id + 1 - 2 * odd,
        frame_id - 4, frame_id + 4, frame_id - 1 + 2 * odd,
    )
    buf, halo, q, do, grad_zb, grad_resid, gain = fetch(
        quant_level, tokens, cotangent[0], quant_scale, shared_proj, output_proj, conv_taps, frames
    )
    kinds = jnp.zeros((2,), jnp.int32)
    for kind, source in enumerate(sources):
        kinds = jnp.where(own_refs == source, kind, kinds)
    rest = jnp.stack([windows[0], row_id, jnp.int32(total_rows)]).astype(jnp.int32)
    meta = jnp.concatenate([kinds, rest])
    residual, hidden, grad_latents, partial, grad_shared, grad_values, grad_output = attention(
        meta, buf, halo, tokens, q, do, grad_resid, shared_proj, value_proj, output_proj
    )
    hidden_ext = row_halo(hidden.reshape(grid), row_id, 1).reshape(-1, width)
    context = residual
    for t in range(3):
        context = context + mm(hidden_ext[t * COLS : (t + rows_dev) * COLS], conv_taps[t])
    coded = (context * gain).astype(BF)

    partial = partial.reshape(2, ext_rows, COLS, width)
    upper = partial[:, :WMAX]
    lower = partial[:, WMAX + rows_dev :]
    got = from_partner(jnp.where(row_id == 0, lower, upper).astype(BF)).astype(F32)
    filler = jnp.zeros((2, rows_dev - WMAX, COLS, width), F32)
    middle = (
        partial[:, WMAX : WMAX + rows_dev]
        + jnp.concatenate([jnp.where(row_id == 0, 0.0, got), filler], axis=1)
        + jnp.concatenate([filler, jnp.where(row_id == 0, got, 0.0)], axis=1)
    )
    targets = (
        frame_id + 2, frame_id - 2, frame_id + 1 - 2 * odd,
        frame_id + 4, frame_id - 4, frame_id - 1 + 2 * odd,
    )
    outgoing = jnp.stack(
        [
            jnp.sum(jnp.where((own_refs == t).reshape(2, 1, 1, 1), middle, 0.0), axis=0)
            .astype(BF)
            .reshape(-1, width)
            for t in targets
        ]
    )
    grad_taps = jnp.stack(
        [mm(hidden_ext[t * COLS : (t + rows_dev) * COLS], grad_zb, 0, 0) for t in range(3)]
    )
    stacked = jnp.concatenate(
        [grad_shared, grad_values, grad_output, grad_taps.reshape(-1, width)], axis=0
    )
    grads = stacked.reshape(2, frames, stacked.shape[0] // (2 * frames), width)
    new_latents, summed = reduce(outgoing, grad_latents, grads, frames)
    norm = 1.0 / math.sqrt(frames * total_rows * COLS)
    summed = summed.reshape(-1, width).astype(F32) * norm
    return (
        coded[None],
        new_latents[None],
        summed[:width],
        summed[width : 2 * width],
        summed[2 * width : 3 * width],
        summed[3 * width :].reshape(3, width, width),
    )


def solution(mesh):
    tok = P(("groups", "frame"), "row", None)
    frm = P(("groups", "frame"))
    placed = (tok, P(("groups", "frame"), None), frm, frm, P(), P(), P(), P(), P(), tok)
    return jax.shard_map(
        local,
        mesh=mesh,
        in_specs=placed,
        out_specs=(
            tok, tok, P("groups", None), P("groups", None), P("groups", None),
            P("groups", None, None),
        ),
        check_vma=False,
    )
```

```python
import functools
import math

import jax
import jax.numpy as jnp
from jax import lax
from jax.experimental import pallas as pl
from jax.experimental.pallas import tpu as pltpu
from jax.sharding import PartitionSpec as P

HEADS = 8
DH = 32
COLS = 64
WMAX = 2
RING = 3
KINDS = 6

SCORE_SCALE = 1.5 / math.sqrt(DH)
LOG2E = math.log2(math.e)
BF = jnp.bfloat16
F32 = jnp.float32
MESH = pl.DeviceIdType.MESH


def mm(a, b, ca=1, cb=0):
    return lax.dot_general(a, b, (((ca,), (cb,)), ((), ())), preferred_element_type=F32)


HALF = 4


def masked_rows(block, f0):
    lane = lax.broadcasted_iota(jnp.int32, (1, HALF * DH), 1) // DH
    part = block[:, f0 : f0 + HALF * DH]
    return jnp.concatenate(
        [jnp.where(lane == h, part, jnp.zeros_like(part)) for h in range(HALF)], axis=0
    )


def head_diagonal(wide):
    rows = wide.T
    lane = lax.broadcasted_iota(jnp.int32, (1, HALF * DH), 1) // DH
    out = rows[:COLS]
    for h in range(1, HALF):
        out = jnp.where(lane == h, rows[h * COLS : (h + 1) * COLS], out)
    return out


def forward_row(i, bias, k_ref, qm_ref, p_ref, pb_ref, inv_ref):
    band = 2 * COLS
    reach = 2 * WMAX + 1
    wide = HALF * COLS
    base = i * band
    kk = SCORE_SCALE * LOG2E
    for hf in range(2):
        f0 = hf * HALF * DH
        ft = slice(f0, f0 + HALF * DH)
        p_ref[i, hf] = mm(k_ref[base : base + reach * band, ft], qm_ref[i, hf], 1, 1)
        m8 = None
        for c in range(reach):
            x = p_ref[i, hf, c * band : (c + 1) * band, :].reshape(band // 8, 8, wide)
            top = jnp.max(x, axis=0) + bias[c]
            m8 = top if m8 is None else jnp.maximum(m8, top)
        m = jnp.max(m8, axis=0, keepdims=True)
        l8 = jnp.zeros((8, wide), F32)
        for c in range(reach):
            sl = slice(c * band, (c + 1) * band)
            p = jnp.exp2(p_ref[i, hf, sl, :] * kk + (bias[c] - m) * kk)
            p_ref[i, hf, sl, :] = p
            l8 = l8 + jnp.sum(p.reshape(band // 8, 8, wide), axis=0)
        inv = 1.0 / jnp.sum(l8, axis=0, keepdims=True)
        inv_ref[i, hf] = inv
        for c in range(reach):
            sl = slice(c * band, (c + 1) * band)
            pb_ref[i, hf, sl, :] = (p_ref[i, hf, sl, :] * inv).astype(BF)


def mix_row(i, vt_ref, pb_ref, mix_ref):
    band = 2 * COLS
    reach = 2 * WMAX + 1
    base = i * band
    for hf in range(2):
        f0 = hf * HALF * DH
        ft = slice(f0, f0 + HALF * DH)
        mix = mm(vt_ref[ft, base : base + reach * band], pb_ref[i, hf])
        mix_ref[i * COLS : (i + 1) * COLS, ft] = head_diagonal(mix).astype(BF)


def score_row(i, v_ref, dom_ref, p_ref, inv_ref, dp_ref, ds_ref):
    band = 2 * COLS
    reach = 2 * WMAX + 1
    wide = HALF * COLS
    base = i * band
    win = slice(base, base + reach * band)
    for hf in range(2):
        f0 = hf * HALF * DH
        ft = slice(f0, f0 + HALF * DH)
        dp_ref[i % RING, hf] = mm(v_ref[win, ft], dom_ref[i, hf], 1, 1)
        u8 = jnp.zeros((8, wide), F32)
        for c in range(reach):
            sl = slice(c * band, (c + 1) * band)
            x = p_ref[i, hf, sl, :] * dp_ref[i % RING, hf, sl, :]
            u8 = u8 + jnp.sum(x.reshape(band // 8, 8, wide), axis=0)
        inv = inv_ref[i, hf]
        ci = inv * SCORE_SCALE
        inner = jnp.sum(u8, axis=0, keepdims=True) * inv * ci
        for c in range(reach):
            sl = slice(c * band, (c + 1) * band)
            ds_ref[i % RING, hf, sl, :] = (p_ref[i, hf, sl, :] * (dp_ref[i % RING, hf, sl, :] * ci - inner)).astype(BF)


def query_row(i, kt_ref, ds_ref, dq_ref):
    band = 2 * COLS
    base = i * band
    win = slice(base, base + (2 * WMAX + 1) * band)
    for hf in range(2):
        f0 = hf * HALF * DH
        ft = slice(f0, f0 + HALF * DH)
        dq = mm(kt_ref[ft, win], ds_ref[i % RING, hf])
        dq_ref[i * COLS : (i + 1) * COLS, ft] = head_diagonal(dq).astype(BF)


def key_row(i, qm_ref, dom_ref, pb_ref, ds_ref, dk_ref, dv_ref):
    band = 2 * COLS
    base = i * band
    win = slice(base, base + (2 * WMAX + 1) * band)
    for hf in range(2):
        f0 = hf * HALF * DH
        ft = slice(f0, f0 + HALF * DH)
        dk_ref[win, ft] += mm(ds_ref[i % RING, hf], qm_ref[i, hf])
        dv_ref[win, ft] += mm(pb_ref[i, hf], dom_ref[i, hf])


def loop(first, last, body):
    lax.fori_loop(first, last, lambda k, carry: (body(k), carry)[1], 0)


class Sum:
    def __init__(self, refs, f, r, frames):
        (self.w, self.p, self.xs, self.xr, self.zw, self.zs, self.zr, self.res,
         self.one, self.zss, self.zsr, self.gs, self.gr) = refs
        self.n = frames // 2
        self.r, self.odd, self.me = r, lax.rem(f, 2), f // 2
        self.across = {"frame": f + 1 - 2 * self.odd}
        self.partner = {"row": 1 - r}

    def link(self, i, source, target, device):
        return pltpu.make_async_remote_copy(
            source, target, self.one.at[2 * i], self.one.at[2 * i + 1],
            device_id=device, device_id_type=MESH,
        )

    def pair(self):
        return self.link(0, self.w.at[1 - self.r], self.p, self.partner)

    def cross(self):
        return self.link(1, self.xs, self.xr, self.across)

    def cross_back(self):
        part = self.res.at[self.r, self.odd]
        return self.link(2, part, part, self.across)

    def pair_back(self, i):
        side = self.odd if i == 0 else 1 - self.odd
        part = self.res.at[self.r, side]
        return self.link(3 + i, part, part, self.partner)

    def scatter(self, k, incoming):
        other = lax.rem(self.me + k, self.n)
        if incoming:
            return pltpu.make_async_remote_copy(
                self.zs.at[other], self.zr.at[other], self.zss.at[k], self.zsr.at[other],
                device_id={"frame": 2 * other + self.odd}, device_id_type=MESH,
            )
        return pltpu.make_async_remote_copy(
            self.zs.at[other], self.zr.at[self.me], self.zss.at[k], self.zsr.at[self.me],
            device_id={"frame": 2 * other + self.odd}, device_id_type=MESH,
        )

    def gather(self, k, incoming):
        other = lax.rem(self.me + k, self.n)
        slot = other if incoming else self.me
        part = self.res.at[self.r, self.odd, slot]
        return pltpu.make_async_remote_copy(
            part, part, self.gs.at[k], self.gr.at[slot],
            device_id={"frame": 2 * other + self.odd}, device_id_type=MESH,
        )

    def begin(self):
        self.pair().start()

    def send_cross(self):
        self.pair().wait()
        away = 1 - self.odd
        self.xs[...] = (self.w[self.r, away] + self.p[away]).astype(BF)
        self.cross().start()

    def send_pieces(self):
        self.cross().wait()
        total = self.w[self.r, self.odd] + self.p[self.odd] + self.xr[...].astype(F32)
        size = total.shape[0] // self.n
        for j in range(self.n):
            piece = total[j * size : (j + 1) * size]
            self.zw[j] = piece
            self.zs[j] = piece.astype(BF)
        loop(1, self.n, lambda k: self.scatter(k, False).start())

    def send_totals(self):
        def add(k, total):
            self.scatter(k, True).wait_recv()
            return total + self.zr[lax.rem(self.me + k, self.n)].astype(F32)

        total = lax.fori_loop(1, self.n, add, self.zw[self.me])
        self.res[self.r, self.odd, self.me] = total.astype(BF)
        loop(1, self.n, lambda k: self.gather(k, False).start())

    def send_back(self):
        loop(1, self.n, lambda k: self.gather(k, True).wait_recv())
        self.cross_back().start()
        self.pair_back(0).start()

    def send_other(self):
        self.cross_back().wait_recv()
        self.pair_back(1).start()

    def finish(self):
        self.pair_back(0).wait()
        self.pair_back(1).wait()
        self.cross_back().wait_send()

        def sent(k):
            self.scatter(k, False).wait_send()
            self.gather(k, False).wait_send()

        loop(1, self.n, sent)

    def quarter(self, half, side):
        return jnp.concatenate(
            [self.res[half, side, j].astype(F32) for j in range(self.n)], axis=0
        )


def codec_kernel(
    frames, refs_ref, window_ref, level_ref, x_ref, ct_ref, qs_ref, sp_ref, vp_ref, op_ref, taps_ref,
    coded_ref, lat_ref, gs_ref, gv_ref, go_ref, gt_ref,
    buf_ref, halo_ref, q_ref, do_ref, gp_ref, resid_ref, cth_ref, ext_ref,
    xi_ref, k_ref, v_ref, kt_ref, vt_ref, mix_ref, dq_ref, dk_ref, dv_ref,
    p_ref, pb_ref, inv_ref, dp_ref, ds_ref, qm_ref, dom_ref,
    residual_ref, hx_ref, eh_ref, ph_ref, pg_ref, out_ref, rb_ref, sb_ref,
    ssem, rsem, hs, hr, bs, br, one,
    *sums,
):
    f = lax.axis_index("frame")
    r = lax.axis_index("row")
    tokens, width = x_ref.shape
    rows = tokens // COLS
    rim = WMAX * COLS
    step = rim
    chunks = tokens // step
    total_rows = rows * lax.axis_size("row")
    odd = lax.rem(f, 2)
    pair = f + 1 - 2 * odd
    lo2, hi2, lo4, hi4 = f >= 2, f + 2 < frames, f >= 4, f + 4 < frames
    side = ((odd == 1) & (f + 1 < frames)) | ((odd == 0) & (f >= 1))
    relay = ((odd == 1) & lo2) | ((odd == 0) & hi2)
    always = f >= 0
    partner = {"row": 1 - r}
    up, down, across = {"frame": f + 2}, {"frame": f - 2}, {"frame": pair}
    weights = Sum(sums[:13], f, r, frames)
    projections = Sum(sums[13:], f, r, frames)

    barrier = pltpu.get_barrier_semaphore()
    pl.semaphore_signal(barrier, inc=1, device_id=partner, device_id_type=MESH)
    pl.semaphore_signal(barrier, inc=1, device_id=across, device_id_type=MESH)

    def hello(k):
        other = {"frame": lax.rem(f + 2 * k, frames)}
        pl.semaphore_signal(barrier, inc=1, device_id=other, device_id_type=MESH)

    loop(1, frames // 2, hello)
    pl.semaphore_wait(barrier, frames // 2 + 1)

    def link(i, source, target, device):
        return pltpu.make_async_remote_copy(
            source, target, one.at[2 * i], one.at[2 * i + 1],
            device_id=device, device_id_type=MESH,
        )

    def place(c):
        return pl.multiple_of(jnp.where(r == 0, chunks - 1 - c, c) * step, step)

    edge = pl.multiple_of((1 - r) * (tokens - COLS), COLS)
    ct_copy = link(0, ct_ref.at[pl.ds(edge, COLS)], cth_ref, partner)
    ct_copy.start()

    def copy(kind, c, source, device):
        part = pl.ds(place(c), step)
        return pltpu.make_async_remote_copy(
            source.at[part], buf_ref.at[kind, part], ssem.at[kind, c], rsem.at[kind, c],
            device_id=device, device_id_type=MESH,
        )

    def halo(kind):
        return pltpu.make_async_remote_copy(
            buf_ref.at[kind, pl.ds(place(0), rim)], halo_ref.at[kind], hs.at[kind], hr.at[kind],
            device_id=partner, device_id_type=MESH,
        )

    have = (lo2, hi2, always, lo4, hi4, side)
    for c in range(chunks):

        @pl.when(hi2)
        def _():
            copy(0, c, x_ref, up).start()

        @pl.when(lo2)
        def _():
            copy(1, c, x_ref, down).start()

        copy(2, c, x_ref, across).start()

    def pass_on(c):
        @pl.when(lo2)
        def _():
            copy(0, c, x_ref, across).wait_recv()
            if c == 0:
                halo(0).start()

        @pl.when(lo2 & hi2)
        def _():
            copy(3, c, buf_ref.at[0], up).start()

        @pl.when(lo2 & (odd == 1))
        def _():
            copy(5, c, buf_ref.at[0], across).start()

        @pl.when(hi2)
        def _():
            copy(1, c, x_ref, across).wait_recv()
            if c == 0:
                halo(1).start()

        @pl.when(hi2 & lo2)
        def _():
            copy(4, c, buf_ref.at[1], down).start()

        @pl.when(hi2 & (odd == 0))
        def _():
            copy(5, c, buf_ref.at[1], across).start()

    level = lax.broadcasted_iota(jnp.int32, (qs_ref.shape[0], 1), 0)
    gain = jnp.sum(
        jnp.where(level == level_ref[0], qs_ref[...], 0.0), axis=0, keepdims=True
    )
    q_ref[...] = mm(x_ref[...], sp_ref[...]).astype(BF)
    grad_z = ct_ref[...].astype(F32) * gain
    resid_ref[...] = grad_z
    grad_zb = grad_z.astype(BF)
    gp_ref[: 2 * COLS, :] = jnp.zeros((2 * COLS, width), BF)
    gp_ref[2 * COLS : 2 * COLS + tokens, :] = grad_zb
    gp_ref[2 * COLS + tokens :, :] = jnp.zeros((2 * COLS, width), BF)
    ext_ref[COLS : COLS + tokens, :] = grad_zb
    dk_ref[...] = jnp.zeros_like(dk_ref)
    dv_ref[...] = jnp.zeros_like(dv_ref)
    got = (lo2, hi2, always, lo2 & hi2, lo2 & hi2, relay)
    for kind in (0, 1, 3, 4, 5):

        @pl.when(jnp.logical_not(got[kind]))
        def _():
            rb_ref[kind, :, :] = jnp.zeros((tokens, width), BF)

    ct_copy.wait()
    outer = (cth_ref[...].astype(F32) * gain).astype(BF)
    blank = jnp.zeros_like(outer)
    ext_ref[:COLS, :] = jnp.where(r == 0, blank, outer)
    ext_ref[COLS + tokens :, :] = jnp.where(r == 0, outer, blank)
    pass_on(0)
    resid = resid_ref[...]
    for t in range(3):
        resid = resid + mm(ext_ref[(2 - t) * COLS : (2 - t) * COLS + tokens, :], taps_ref[t], 1, 1)
    resid_ref[...] = resid
    pass_on(1)
    do_ref[...] = mm(resid_ref[...].astype(BF), op_ref[...], 1, 1).astype(BF)
    copy(2, 0, x_ref, across).wait_recv()
    halo(2).start()
    for c in range(2, chunks):
        pass_on(c)
    for i in range(rows):
        tok = slice(i * COLS, (i + 1) * COLS)
        for hf in range(2):
            qm_ref[i, hf] = masked_rows(q_ref[tok, :], hf * HALF * DH)
            dom_ref[i, hf] = masked_rows(do_ref[tok, :], hf * HALF * DH)
    for c in range(chunks):
        for kind in range(2, KINDS):
            if kind > 2 or c:

                @pl.when(have[kind])
                def _():
                    copy(kind, c, x_ref, across).wait_recv()
                    if c == 0:
                        halo(kind).start()

    for kind in range(KINDS):

        @pl.when(have[kind])
        def _():
            halo(kind).wait()

    sources = (f - 2, f + 2, pair, f - 4, f + 4, f - 1 + 2 * odd)
    targets = (f + 2, f - 2, pair, f + 4, f - 4, f - 1 + 2 * odd)
    for s in range(2):
        own = refs_ref[0, s]
        kind = jnp.int32(0)
        for number, source in enumerate(sources):
            kind = jnp.where(own == source, number, kind)
        for e in range(rows):
            at = (2 * (e + WMAX) + s) * COLS
            xi_ref[at : at + COLS, :] = buf_ref[kind, e * COLS : (e + 1) * COLS, :]
        for e in range(WMAX):
            piece = halo_ref[kind, e * COLS : (e + 1) * COLS, :]
            none = jnp.zeros_like(piece)
            at = (2 * e + s) * COLS
            xi_ref[at : at + COLS, :] = jnp.where(r == 0, none, piece)
            at = (2 * (e + WMAX + rows) + s) * COLS
            xi_ref[at : at + COLS, :] = jnp.where(r == 0, piece, none)

    keys = mm(xi_ref[...], sp_ref[...]).astype(BF)
    k_ref[...] = keys
    kt_ref[...] = keys.T
    vals = mm(xi_ref[...], vp_ref[...]).astype(BF)
    v_ref[...] = vals
    vt_ref[...] = vals.T
    first_row = r * rows
    window = window_ref[0]

    def bias_of(i):
        out = []
        for c in range(2 * WMAX + 1):
            key_row = first_row + i + c - WMAX
            inside = (key_row >= 0) & (key_row < total_rows) & (abs(c - WMAX) <= window)
            out.append(jnp.where(inside, 0.0, -jnp.inf).astype(F32))
        return out

    for i in range(rows):
        forward_row(i, bias_of(i), k_ref, qm_ref, p_ref, pb_ref, inv_ref)
    for i in range(rows):
        mix_row(i, vt_ref, pb_ref, mix_ref)

    residual = x_ref[...].astype(F32) + mm(mix_ref[...], op_ref[...])
    residual_ref[...] = residual
    hx_ref[COLS : COLS + tokens, :] = residual.astype(BF)
    inner = pl.multiple_of(COLS + (1 - r) * (tokens - COLS), COLS)
    hidden_copy = link(1, hx_ref.at[pl.ds(inner, COLS)], eh_ref, partner)
    hidden_copy.start()
    weights.w[0, 0] = mm(mix_ref[...].T, resid_ref[...].astype(BF))
    hidden_copy.wait()
    outer = eh_ref[...]
    blank = jnp.zeros_like(outer)
    hx_ref[:COLS, :] = jnp.where(r == 0, blank, outer)
    hx_ref[COLS + tokens :, :] = jnp.where(r == 0, outer, blank)
    hxt = hx_ref[...].T
    span = tokens + 2 * COLS
    for t in range(3):
        weights.w[(t + 1) // 2, (t + 1) % 2] = mm(hxt, gp_ref[(2 - t) * COLS : (2 - t) * COLS + span, :])
    weights.begin()

    for i in range(rows + 1):
        if i == 2:
            weights.send_cross()
        if i == 6:
            weights.send_pieces()
        if i < rows:
            score_row(i, v_ref, dom_ref, p_ref, inv_ref, dp_ref, ds_ref)
        if i:
            key_row(i - 1, qm_ref, dom_ref, pb_ref, ds_ref, dk_ref, dv_ref)
            query_row(i - 1, kt_ref, ds_ref, dq_ref)

    def project(at):
        return mm(dk_ref[pl.ds(at, 2 * step), :].astype(BF), sp_ref[...], 1, 1) + mm(
            dv_ref[pl.ds(at, 2 * step), :].astype(BF), vp_ref[...], 1, 1
        )

    ph_ref[...] = project(
        pl.multiple_of(jnp.where(r == 0, 2 * (tokens + rim), 0), 2 * step)
    ).astype(BF)
    part_copy = link(2, ph_ref, pg_ref, partner)
    part_copy.start()

    sent = (hi2, lo2, always, hi4, lo4, side)
    device = (up, down, across, up, down, across)

    def give(kind, c, source):
        part = pl.ds(place(c), step)
        return pltpu.make_async_remote_copy(
            source.at[part], rb_ref.at[kind, part], bs.at[kind, c], br.at[kind, c],
            device_id=device[kind], device_id_type=MESH,
        )

    def hand_out(c):
        at = place(c)
        block = project(pl.multiple_of(2 * at + 2 * rim, 2 * step))
        if c == 0:
            block = block + pg_ref[...].astype(F32)
        for kind, target in enumerate(targets):
            first = refs_ref[0, 0] == target
            second = refs_ref[0, 1] == target
            for e in range(WMAX):
                part = jnp.where(first, block[2 * e * COLS : (2 * e + 1) * COLS], 0.0)
                part = part + jnp.where(second, block[(2 * e + 1) * COLS : (2 * e + 2) * COLS], 0.0)
                out_ref[kind, pl.ds(pl.multiple_of(at + e * COLS, COLS), COLS), :] = part.astype(BF)
        for kind in (3, 4, 5, 2):

            @pl.when(sent[kind])
            def _():
                give(kind, c, out_ref.at[kind]).start()

    even = jnp.where(odd == 0, 1.0, 0.0).astype(F32)

    def merge(c):
        for kind in (3, 4, 5):

            @pl.when(got[kind])
            def _():
                give(kind, c, out_ref.at[kind]).wait_recv()

        part = pl.ds(place(c), step)
        extra = rb_ref[5, part, :].astype(F32)
        rising = out_ref[0, part, :].astype(F32) + rb_ref[3, part, :].astype(F32) + extra * even
        falling = (
            out_ref[1, part, :].astype(F32) + rb_ref[4, part, :].astype(F32) + extra * (1.0 - even)
        )
        sb_ref[0, part, :] = rising.astype(BF)
        sb_ref[1, part, :] = falling.astype(BF)

        @pl.when(hi2)
        def _():
            give(0, c, sb_ref.at[0]).start()

        @pl.when(lo2)
        def _():
            give(1, c, sb_ref.at[1]).start()

    def collect(c):
        for kind in (0, 1, 2):

            @pl.when(got[kind])
            def _():
                give(kind, c, out_ref.at[kind]).wait_recv()

        part = pl.ds(place(c), step)
        lat_ref[part, :] = (
            resid_ref[part, :]
            + rb_ref[0, part, :].astype(F32)
            + rb_ref[1, part, :].astype(F32)
            + rb_ref[2, part, :].astype(F32)
        ).astype(BF)

    order = tuple(reversed(range(chunks)))
    for c in order[:-1]:
        hand_out(c)
    part_copy.wait()
    hand_out(0)
    weights.send_totals()
    xit = xi_ref[...].T
    grad_shared = mm(x_ref[...].T, dq_ref[...]) + mm(xit, dk_ref[...].astype(BF))
    grad_values = mm(xit, dv_ref[...].astype(BF))
    half = width // 2
    for s in range(2):
        projections.w[0, s] = grad_shared[s * half : (s + 1) * half]
        projections.w[1, s] = grad_values[s * half : (s + 1) * half]
    projections.begin()
    merge(order[0])
    projections.send_cross()
    merge(order[1])
    weights.send_back()
    resid_ref[...] = resid_ref[...] + mm(dq_ref[...], sp_ref[...], 1, 1)
    context = residual_ref[...]
    for t in range(3):
        context = context + mm(hx_ref[t * COLS : t * COLS + tokens, :], taps_ref[t])
    coded_ref[...] = (context * gain).astype(BF)
    projections.send_pieces()
    merge(order[2])
    weights.send_other()
    projections.send_totals()
    for c in order[3:]:
        merge(c)
    projections.send_back()
    norm = 1.0 / math.sqrt(frames * total_rows * COLS)
    for c in order[:2]:
        collect(c)
    projections.send_other()
    weights.finish()
    go_ref[...] = weights.quarter(0, 0) * norm
    for t in range(3):
        gt_ref[t] = weights.quarter((t + 1) // 2, (t + 1) % 2) * norm
    for c in order[2:]:
        collect(c)
    projections.finish()
    for s in range(2):
        gs_ref[s * half : (s + 1) * half, :] = projections.quarter(0, s) * norm
        gv_ref[s * half : (s + 1) * half, :] = projections.quarter(1, s) * norm

    passed = (hi2, lo2, always, lo2 & hi2, lo2 & hi2, relay)
    for kind in range(KINDS):

        @pl.when(passed[kind])
        def _():
            for c in range(chunks):
                copy(kind, c, x_ref, across).wait_send()

        @pl.when(sent[kind])
        def _():
            for c in range(chunks):
                give(kind, c, out_ref.at[kind]).wait_send()


def sum_scratch(size, width, n):
    dma = pltpu.SemaphoreType.DMA
    return [
        pltpu.VMEM((2, 2, size, width), F32),
        pltpu.VMEM((2, size, width), F32),
        pltpu.VMEM((size, width), BF),
        pltpu.VMEM((size, width), BF),
        pltpu.VMEM((n, size // n, width), F32),
        pltpu.VMEM((n, size // n, width), BF),
        pltpu.VMEM((n, size // n, width), BF),
        pltpu.VMEM((2, 2, n, size // n, width), BF),
        dma((10,)), dma((n,)), dma((n,)), dma((n,)), dma((n,)),
    ]


def local(
    latents, ref_frames, windows, quant_level, quant_scale,
    shared_proj, value_proj, output_proj, conv_taps, cotangent,
):
    tokens, width = latents.shape[1:]
    frames = lax.axis_size("frame")
    rows = tokens // COLS
    ext = tokens + 2 * WMAX * COLS
    keys = 2 * (2 * WMAX + 1) * COLS
    wide = HALF * COLS
    rim = WMAX * COLS
    chunks = tokens // rim
    vm = pl.BlockSpec(memory_space=pltpu.VMEM)
    sm = pl.BlockSpec(memory_space=pltpu.SMEM)
    dma = pltpu.SemaphoreType.DMA
    slab = jax.ShapeDtypeStruct((tokens, width), BF)
    square = jax.ShapeDtypeStruct((width, width), F32)

    def rows_of(count, kind=BF):
        return pltpu.VMEM((count, width), kind)

    coded, grad_latents, grad_shared, grad_values, grad_output, grad_taps = pl.pallas_call(
        functools.partial(codec_kernel, frames),
        out_shape=(
            slab, slab, square, square, square, jax.ShapeDtypeStruct((3, width, width), F32),
        ),
        in_specs=[sm] * 3 + [vm] * 7,
        out_specs=(vm,) * 6,
        scratch_shapes=[
            pltpu.VMEM((KINDS, tokens, width), BF),
            pltpu.VMEM((KINDS, rim, width), BF),
            rows_of(tokens), rows_of(tokens), rows_of(tokens + 4 * COLS), rows_of(tokens, F32),
            rows_of(COLS), rows_of(tokens + 2 * COLS),
            rows_of(2 * ext), rows_of(2 * ext), rows_of(2 * ext),
            pltpu.VMEM((width, 2 * ext), BF),
            pltpu.VMEM((width, 2 * ext), BF),
            rows_of(tokens), rows_of(tokens), rows_of(2 * ext, F32), rows_of(2 * ext, F32),
            pltpu.VMEM((rows, 2, keys, wide), F32),
            pltpu.VMEM((rows, 2, keys, wide), BF),
            pltpu.VMEM((rows, 2, 1, wide), F32),
            pltpu.VMEM((RING, 2, keys, wide), F32),
            pltpu.VMEM((RING, 2, keys, wide), BF),
            pltpu.VMEM((rows, 2, wide, HALF * DH), BF),
            pltpu.VMEM((rows, 2, wide, HALF * DH), BF),
            rows_of(tokens, F32), rows_of(tokens + 2 * COLS), rows_of(COLS),
            rows_of(2 * rim), rows_of(2 * rim),
            pltpu.VMEM((KINDS, tokens, width), BF),
            pltpu.VMEM((KINDS, tokens, width), BF),
            pltpu.VMEM((2, tokens, width), BF),
            dma((KINDS, chunks)), dma((KINDS, chunks)), dma((KINDS,)), dma((KINDS,)),
            dma((KINDS, chunks)), dma((KINDS, chunks)), dma((6,)),
        ]
        + sum_scratch(width, width, frames // 2)
        + sum_scratch(width // 2, width, frames // 2),
        compiler_params=pltpu.CompilerParams(
            collective_id=0, has_side_effects=True, vmem_limit_bytes=62_000_000
        ),
        name="codec",
    )(
        ref_frames, windows, quant_level, latents[0], cotangent[0], quant_scale,
        shared_proj, value_proj, output_proj, conv_taps,
    )
    return (
        coded[None], grad_latents[None], grad_shared, grad_values, grad_output, grad_taps
    )


def solution(mesh):
    tok = P(("groups", "frame"), "row", None)
    frm = P(("groups", "frame"))
    placed = (tok, P(("groups", "frame"), None), frm, frm, P(), P(), P(), P(), P(), tok)
    return jax.shard_map(
        local,
        mesh=mesh,
        in_specs=placed,
        out_specs=(
            tok, tok, P("groups", None), P("groups", None), P("groups", None),
            P("groups", None, None),
        ),
        check_vma=False,
    )
```

```python
import functools
import math

import jax
import jax.numpy as jnp
from jax import lax
from jax.experimental import pallas as pl
from jax.experimental.pallas import tpu as pltpu
from jax.sharding import PartitionSpec as P

HEADS = 8
DH = 32
COLS = 64
WMAX = 2
RING = 3
KINDS = 6

SCORE_SCALE = 1.5 / math.sqrt(DH)
LOG2E = math.log2(math.e)
BF = jnp.bfloat16
F32 = jnp.float32
MESH = pl.DeviceIdType.MESH


def mm(a, b, ca=1, cb=0):
    return lax.dot_general(a, b, (((ca,), (cb,)), ((), ())), preferred_element_type=F32)


HALF = 4


def masked_rows(block, f0):
    lane = lax.broadcasted_iota(jnp.int32, (1, HALF * DH), 1) // DH
    part = block[:, f0 : f0 + HALF * DH]
    return jnp.concatenate(
        [jnp.where(lane == h, part, jnp.zeros_like(part)) for h in range(HALF)], axis=0
    )


def head_diagonal(wide):
    rows = wide.T
    lane = lax.broadcasted_iota(jnp.int32, (1, HALF * DH), 1) // DH
    out = rows[:COLS]
    for h in range(1, HALF):
        out = jnp.where(lane == h, rows[h * COLS : (h + 1) * COLS], out)
    return out


def forward_row(i, bias, k_ref, qm_ref, p_ref, pb_ref, inv_ref):
    band = 2 * COLS
    reach = 2 * WMAX + 1
    wide = HALF * COLS
    base = i * band
    kk = SCORE_SCALE * LOG2E
    for hf in range(2):
        f0 = hf * HALF * DH
        ft = slice(f0, f0 + HALF * DH)
        p_ref[i, hf] = mm(k_ref[base : base + reach * band, ft], qm_ref[i, hf], 1, 1)
        m8 = None
        for c in range(reach):
            x = p_ref[i, hf, c * band : (c + 1) * band, :].reshape(band // 8, 8, wide)
            top = jnp.max(x, axis=0) + bias[c]
            m8 = top if m8 is None else jnp.maximum(m8, top)
        m = jnp.max(m8, axis=0, keepdims=True)
        l8 = jnp.zeros((8, wide), F32)
        for c in range(reach):
            sl = slice(c * band, (c + 1) * band)
            p = jnp.exp2(p_ref[i, hf, sl, :] * kk + (bias[c] - m) * kk)
            p_ref[i, hf, sl, :] = p
            l8 = l8 + jnp.sum(p.reshape(band // 8, 8, wide), axis=0)
        inv = 1.0 / jnp.sum(l8, axis=0, keepdims=True)
        inv_ref[i, hf] = inv
        for c in range(reach):
            sl = slice(c * band, (c + 1) * band)
            pb_ref[i, hf, sl, :] = (p_ref[i, hf, sl, :] * inv).astype(BF)


def mix_row(i, vt_ref, pb_ref, mix_ref):
    band = 2 * COLS
    reach = 2 * WMAX + 1
    base = i * band
    for hf in range(2):
        f0 = hf * HALF * DH
        ft = slice(f0, f0 + HALF * DH)
        mix = mm(vt_ref[ft, base : base + reach * band], pb_ref[i, hf])
        mix_ref[i * COLS : (i + 1) * COLS, ft] = head_diagonal(mix).astype(BF)


def score_row(i, v_ref, dom_ref, p_ref, inv_ref, dp_ref, ds_ref):
    band = 2 * COLS
    reach = 2 * WMAX + 1
    wide = HALF * COLS
    base = i * band
    win = slice(base, base + reach * band)
    for hf in range(2):
        f0 = hf * HALF * DH
        ft = slice(f0, f0 + HALF * DH)
        dp_ref[i % RING, hf] = mm(v_ref[win, ft], dom_ref[i, hf], 1, 1)
        u8 = jnp.zeros((8, wide), F32)
        for c in range(reach):
            sl = slice(c * band, (c + 1) * band)
            x = p_ref[i, hf, sl, :] * dp_ref[i % RING, hf, sl, :]
            u8 = u8 + jnp.sum(x.reshape(band // 8, 8, wide), axis=0)
        inv = inv_ref[i, hf]
        ci = inv * SCORE_SCALE
        inner = jnp.sum(u8, axis=0, keepdims=True) * inv * ci
        for c in range(reach):
            sl = slice(c * band, (c + 1) * band)
            ds_ref[i % RING, hf, sl, :] = (p_ref[i, hf, sl, :] * (dp_ref[i % RING, hf, sl, :] * ci - inner)).astype(BF)


def query_row(i, kt_ref, ds_ref, dq_ref):
    band = 2 * COLS
    base = i * band
    win = slice(base, base + (2 * WMAX + 1) * band)
    for hf in range(2):
        f0 = hf * HALF * DH
        ft = slice(f0, f0 + HALF * DH)
        dq = mm(kt_ref[ft, win], ds_ref[i % RING, hf])
        dq_ref[i * COLS : (i + 1) * COLS, ft] = head_diagonal(dq).astype(BF)


def key_row(i, qm_ref, dom_ref, pb_ref, ds_ref, dk_ref, dv_ref):
    band = 2 * COLS
    base = i * band
    win = slice(base, base + (2 * WMAX + 1) * band)
    for hf in range(2):
        f0 = hf * HALF * DH
        ft = slice(f0, f0 + HALF * DH)
        dk_ref[win, ft] += mm(ds_ref[i % RING, hf], qm_ref[i, hf])
        dv_ref[win, ft] += mm(pb_ref[i, hf], dom_ref[i, hf])


def loop(first, last, body):
    lax.fori_loop(first, last, lambda k, carry: (body(k), carry)[1], 0)


class Sum:
    def __init__(self, refs, res, f, r, frames):
        (self.w, self.p, self.xs, self.xr, self.zw, self.zs, self.zr,
         self.one, self.zss, self.zsr, self.gs, self.gr) = refs
        self.res = res
        self.n = frames // 2
        self.r, self.odd, self.me = r, lax.rem(f, 2), f // 2
        self.across = {"frame": f + 1 - 2 * self.odd}
        self.partner = {"row": 1 - r}

    def link(self, i, source, target, device):
        return pltpu.make_async_remote_copy(
            source, target, self.one.at[2 * i], self.one.at[2 * i + 1],
            device_id=device, device_id_type=MESH,
        )

    def pair(self):
        return self.link(0, self.w.at[1 - self.r], self.p, self.partner)

    def cross(self):
        return self.link(1, self.xs, self.xr, self.across)

    def cross_back(self):
        part = self.res.at[self.r, self.odd]
        return self.link(2, part, part, self.across)

    def pair_back(self, i):
        side = self.odd if i == 0 else 1 - self.odd
        part = self.res.at[self.r, side]
        return self.link(3 + i, part, part, self.partner)

    def scatter(self, k, incoming):
        other = lax.rem(self.me + k, self.n)
        if incoming:
            return pltpu.make_async_remote_copy(
                self.zs.at[other], self.zr.at[other], self.zss.at[k], self.zsr.at[other],
                device_id={"frame": 2 * other + self.odd}, device_id_type=MESH,
            )
        return pltpu.make_async_remote_copy(
            self.zs.at[other], self.zr.at[self.me], self.zss.at[k], self.zsr.at[self.me],
            device_id={"frame": 2 * other + self.odd}, device_id_type=MESH,
        )

    def gather(self, k, incoming):
        other = lax.rem(self.me + k, self.n)
        slot = other if incoming else self.me
        part = self.res.at[self.r, self.odd, slot]
        return pltpu.make_async_remote_copy(
            part, part, self.gs.at[k], self.gr.at[slot],
            device_id={"frame": 2 * other + self.odd}, device_id_type=MESH,
        )

    def begin(self):
        self.pair().start()

    def send_cross(self):
        self.pair().wait()
        away = 1 - self.odd
        self.xs[...] = (self.w[self.r, away] + self.p[away]).astype(BF)
        self.cross().start()

    def send_pieces(self):
        self.cross().wait()
        total = self.w[self.r, self.odd] + self.p[self.odd] + self.xr[...].astype(F32)
        size = total.shape[0] // self.n
        for j in range(self.n):
            piece = total[j * size : (j + 1) * size]
            self.zw[j] = piece
            self.zs[j] = piece.astype(BF)
        loop(1, self.n, lambda k: self.scatter(k, False).start())

    def send_totals(self):
        def add(k, total):
            self.scatter(k, True).wait_recv()
            return total + self.zr[lax.rem(self.me + k, self.n)].astype(F32)

        total = lax.fori_loop(1, self.n, add, self.zw[self.me])
        self.res[self.r, self.odd, self.me] = total.astype(BF)
        loop(1, self.n, lambda k: self.gather(k, False).start())

    def send_back(self):
        loop(1, self.n, lambda k: self.gather(k, True).wait_recv())
        self.cross_back().start()
        self.pair_back(0).start()

    def send_other(self):
        self.cross_back().wait_recv()
        self.pair_back(1).start()

    def finish(self):
        self.pair_back(0).wait()
        self.pair_back(1).wait()
        self.cross_back().wait_send()

        def sent(k):
            self.scatter(k, False).wait_send()
            self.gather(k, False).wait_send()

        loop(1, self.n, sent)

def codec_kernel(
    frames, refs_ref, window_ref, level_ref, *rest,
):
    inputs, rest = rest[:7], rest[7:]
    (coded_hbm, lat_hbm, wsum_ref, psum_ref), rest = rest[:4], rest[4:]
    held, rest = rest[:9], rest[9:]
    x_ref, ct_ref, qs_ref, sp_ref, vp_ref, op_ref, taps_ref, coded_ref, lat_ref = held
    (
        buf_ref, halo_ref, q_ref, do_ref, gp_ref, resid_ref, cth_ref, ext_ref, xi_ref, k_ref,
        v_ref, kt_ref, vt_ref, mix_ref, dq_ref, dk_ref, dv_ref, p_ref, pb_ref, inv_ref, dp_ref,
        ds_ref, qm_ref, dom_ref, residual_ref, hx_ref, eh_ref, ph_ref, pg_ref, out_ref, rb_ref,
        sb_ref, ssem, rsem, hs, hr, bs, br, one, local_sems,
    ), sums = rest[:40], rest[40:]
    f = lax.axis_index("frame")
    r = lax.axis_index("row")
    tokens, width = x_ref.shape
    rows = tokens // COLS
    rim = WMAX * COLS
    step = rim
    chunks = tokens // step
    total_rows = rows * lax.axis_size("row")
    odd = lax.rem(f, 2)
    pair = f + 1 - 2 * odd
    lo2, hi2, lo4, hi4 = f >= 2, f + 2 < frames, f >= 4, f + 4 < frames
    side = ((odd == 1) & (f + 1 < frames)) | ((odd == 0) & (f >= 1))
    relay = ((odd == 1) & lo2) | ((odd == 0) & hi2)
    always = f >= 0
    partner = {"row": 1 - r}
    up, down, across = {"frame": f + 2}, {"frame": f - 2}, {"frame": pair}
    weights = Sum(sums[:12], wsum_ref, f, r, frames)
    projections = Sum(sums[12:], psum_ref, f, r, frames)

    loads = [
        pltpu.make_async_copy(source, target, local_sems.at[i])
        for i, (source, target) in enumerate(zip(inputs, held))
    ]
    for load in loads:
        load.start()
    barrier = pltpu.get_barrier_semaphore()
    pl.semaphore_signal(barrier, inc=1, device_id=partner, device_id_type=MESH)
    pl.semaphore_signal(barrier, inc=1, device_id=across, device_id_type=MESH)

    def hello(k):
        other = {"frame": lax.rem(f + 2 * k, frames)}
        pl.semaphore_signal(barrier, inc=1, device_id=other, device_id_type=MESH)

    loop(1, frames // 2, hello)
    pl.semaphore_wait(barrier, frames // 2 + 1)

    def link(i, source, target, device):
        return pltpu.make_async_remote_copy(
            source, target, one.at[2 * i], one.at[2 * i + 1],
            device_id=device, device_id_type=MESH,
        )

    def place(c):
        return pl.multiple_of(jnp.where(r == 0, chunks - 1 - c, c) * step, step)

    loads[0].wait()
    edge = pl.multiple_of((1 - r) * (tokens - COLS), COLS)

    def copy(kind, c, source, device):
        part = pl.ds(place(c), step)
        return pltpu.make_async_remote_copy(
            source.at[part], buf_ref.at[kind, part], ssem.at[kind, c], rsem.at[kind, c],
            device_id=device, device_id_type=MESH,
        )

    def halo(kind):
        return pltpu.make_async_remote_copy(
            buf_ref.at[kind, pl.ds(place(0), rim)], halo_ref.at[kind], hs.at[kind], hr.at[kind],
            device_id=partner, device_id_type=MESH,
        )

    have = (lo2, hi2, always, lo4, hi4, side)
    for c in range(chunks):

        @pl.when(hi2)
        def _():
            copy(0, c, x_ref, up).start()

        @pl.when(lo2)
        def _():
            copy(1, c, x_ref, down).start()

        copy(2, c, x_ref, across).start()

    for load in loads[1:]:
        load.wait()
    ct_copy = link(0, ct_ref.at[pl.ds(edge, COLS)], cth_ref, partner)
    ct_copy.start()

    def pass_on(c):
        @pl.when(lo2)
        def _():
            copy(0, c, x_ref, across).wait_recv()
            if c == 0:
                halo(0).start()

        @pl.when(lo2 & hi2)
        def _():
            copy(3, c, buf_ref.at[0], up).start()

        @pl.when(lo2 & (odd == 1))
        def _():
            copy(5, c, buf_ref.at[0], across).start()

        @pl.when(hi2)
        def _():
            copy(1, c, x_ref, across).wait_recv()
            if c == 0:
                halo(1).start()

        @pl.when(hi2 & lo2)
        def _():
            copy(4, c, buf_ref.at[1], down).start()

        @pl.when(hi2 & (odd == 0))
        def _():
            copy(5, c, buf_ref.at[1], across).start()

    level = lax.broadcasted_iota(jnp.int32, (qs_ref.shape[0], 1), 0)
    gain = jnp.sum(
        jnp.where(level == level_ref[0], qs_ref[...], 0.0), axis=0, keepdims=True
    )
    q_ref[...] = mm(x_ref[...], sp_ref[...]).astype(BF)
    grad_z = ct_ref[...].astype(F32) * gain
    resid_ref[...] = grad_z
    grad_zb = grad_z.astype(BF)
    gp_ref[: 2 * COLS, :] = jnp.zeros((2 * COLS, width), BF)
    gp_ref[2 * COLS : 2 * COLS + tokens, :] = grad_zb
    gp_ref[2 * COLS + tokens :, :] = jnp.zeros((2 * COLS, width), BF)
    ext_ref[COLS : COLS + tokens, :] = grad_zb
    dk_ref[...] = jnp.zeros_like(dk_ref)
    dv_ref[...] = jnp.zeros_like(dv_ref)
    got = (lo2, hi2, always, lo2 & hi2, lo2 & hi2, relay)
    for kind in (0, 1, 3, 4, 5):

        @pl.when(jnp.logical_not(got[kind]))
        def _():
            rb_ref[kind, :, :] = jnp.zeros((tokens, width), BF)

    ct_copy.wait()
    outer = (cth_ref[...].astype(F32) * gain).astype(BF)
    blank = jnp.zeros_like(outer)
    ext_ref[:COLS, :] = jnp.where(r == 0, blank, outer)
    ext_ref[COLS + tokens :, :] = jnp.where(r == 0, outer, blank)
    pass_on(0)
    resid = resid_ref[...]
    for t in range(3):
        resid = resid + mm(ext_ref[(2 - t) * COLS : (2 - t) * COLS + tokens, :], taps_ref[t], 1, 1)
    resid_ref[...] = resid
    pass_on(1)
    do_ref[...] = mm(resid_ref[...].astype(BF), op_ref[...], 1, 1).astype(BF)
    copy(2, 0, x_ref, across).wait_recv()
    halo(2).start()
    for c in range(2, chunks):
        pass_on(c)
    for i in range(rows):
        tok = slice(i * COLS, (i + 1) * COLS)
        for hf in range(2):
            qm_ref[i, hf] = masked_rows(q_ref[tok, :], hf * HALF * DH)
            dom_ref[i, hf] = masked_rows(do_ref[tok, :], hf * HALF * DH)
    for c in range(chunks):
        for kind in range(2, KINDS):
            if kind > 2 or c:

                @pl.when(have[kind])
                def _():
                    copy(kind, c, x_ref, across).wait_recv()
                    if c == 0:
                        halo(kind).start()

    for kind in range(KINDS):

        @pl.when(have[kind])
        def _():
            halo(kind).wait()

    sources = (f - 2, f + 2, pair, f - 4, f + 4, f - 1 + 2 * odd)
    targets = (f + 2, f - 2, pair, f + 4, f - 4, f - 1 + 2 * odd)
    for s in range(2):
        own = refs_ref[0, s]
        kind = jnp.int32(0)
        for number, source in enumerate(sources):
            kind = jnp.where(own == source, number, kind)
        for e in range(rows):
            at = (2 * (e + WMAX) + s) * COLS
            xi_ref[at : at + COLS, :] = buf_ref[kind, e * COLS : (e + 1) * COLS, :]
        for e in range(WMAX):
            piece = halo_ref[kind, e * COLS : (e + 1) * COLS, :]
            none = jnp.zeros_like(piece)
            at = (2 * e + s) * COLS
            xi_ref[at : at + COLS, :] = jnp.where(r == 0, none, piece)
            at = (2 * (e + WMAX + rows) + s) * COLS
            xi_ref[at : at + COLS, :] = jnp.where(r == 0, piece, none)

    keys = mm(xi_ref[...], sp_ref[...]).astype(BF)
    k_ref[...] = keys
    kt_ref[...] = keys.T
    vals = mm(xi_ref[...], vp_ref[...]).astype(BF)
    v_ref[...] = vals
    vt_ref[...] = vals.T
    first_row = r * rows
    window = window_ref[0]

    def bias_of(i):
        out = []
        for c in range(2 * WMAX + 1):
            key_row = first_row + i + c - WMAX
            inside = (key_row >= 0) & (key_row < total_rows) & (abs(c - WMAX) <= window)
            out.append(jnp.where(inside, 0.0, -jnp.inf).astype(F32))
        return out

    for i in range(rows):
        forward_row(i, bias_of(i), k_ref, qm_ref, p_ref, pb_ref, inv_ref)
    for i in range(rows):
        mix_row(i, vt_ref, pb_ref, mix_ref)

    residual = x_ref[...].astype(F32) + mm(mix_ref[...], op_ref[...])
    residual_ref[...] = residual
    hx_ref[COLS : COLS + tokens, :] = residual.astype(BF)
    inner = pl.multiple_of(COLS + (1 - r) * (tokens - COLS), COLS)
    hidden_copy = link(1, hx_ref.at[pl.ds(inner, COLS)], eh_ref, partner)
    hidden_copy.start()
    weights.w[0, 0] = mm(mix_ref[...].T, resid_ref[...].astype(BF))
    hidden_copy.wait()
    outer = eh_ref[...]
    blank = jnp.zeros_like(outer)
    hx_ref[:COLS, :] = jnp.where(r == 0, blank, outer)
    hx_ref[COLS + tokens :, :] = jnp.where(r == 0, outer, blank)
    hxt = hx_ref[...].T
    span = tokens + 2 * COLS
    for t in range(3):
        weights.w[(t + 1) // 2, (t + 1) % 2] = mm(hxt, gp_ref[(2 - t) * COLS : (2 - t) * COLS + span, :])
    weights.begin()

    for i in range(rows + 1):
        if i == 2:
            weights.send_cross()
        if i == 6:
            weights.send_pieces()
        if i < rows:
            score_row(i, v_ref, dom_ref, p_ref, inv_ref, dp_ref, ds_ref)
        if i:
            key_row(i - 1, qm_ref, dom_ref, pb_ref, ds_ref, dk_ref, dv_ref)
            query_row(i - 1, kt_ref, ds_ref, dq_ref)

    def project(at):
        return mm(dk_ref[pl.ds(at, 2 * step), :].astype(BF), sp_ref[...], 1, 1) + mm(
            dv_ref[pl.ds(at, 2 * step), :].astype(BF), vp_ref[...], 1, 1
        )

    sent = (hi2, lo2, always, hi4, lo4, side)
    device = (up, down, across, up, down, across)

    def give(kind, c, source):
        part = pl.ds(place(c), step)
        return pltpu.make_async_remote_copy(
            source.at[part], rb_ref.at[kind, part], bs.at[kind, c], br.at[kind, c],
            device_id=device[kind], device_id_type=MESH,
        )

    def hand_out(c):
        at = place(c)
        block = project(pl.multiple_of(2 * at + 2 * rim, 2 * step))
        if c == 0:
            block = block + pg_ref[...].astype(F32)
        for kind, target in enumerate(targets):
            first = refs_ref[0, 0] == target
            second = refs_ref[0, 1] == target
            for e in range(WMAX):
                part = jnp.where(first, block[2 * e * COLS : (2 * e + 1) * COLS], 0.0)
                part = part + jnp.where(second, block[(2 * e + 1) * COLS : (2 * e + 2) * COLS], 0.0)
                out_ref[kind, pl.ds(pl.multiple_of(at + e * COLS, COLS), COLS), :] = part.astype(BF)
        for kind in (3, 4, 5):

            @pl.when(sent[kind])
            def _():
                give(kind, c, out_ref.at[kind]).start()

    even = jnp.where(odd == 0, 1.0, 0.0).astype(F32)

    def merge(c):
        for kind in (3, 4, 5):

            @pl.when(got[kind])
            def _():
                give(kind, c, out_ref.at[kind]).wait_recv()

        give(2, c, out_ref.at[2]).start()
        part = pl.ds(place(c), step)
        extra = rb_ref[5, part, :].astype(F32)
        rising = out_ref[0, part, :].astype(F32) + rb_ref[3, part, :].astype(F32) + extra * even
        falling = (
            out_ref[1, part, :].astype(F32) + rb_ref[4, part, :].astype(F32) + extra * (1.0 - even)
        )
        sb_ref[0, part, :] = rising.astype(BF)
        sb_ref[1, part, :] = falling.astype(BF)

        @pl.when(hi2)
        def _():
            give(0, c, sb_ref.at[0]).start()

        @pl.when(lo2)
        def _():
            give(1, c, sb_ref.at[1]).start()

    def collect(c):
        for kind in (0, 1, 2):

            @pl.when(got[kind])
            def _():
                give(kind, c, out_ref.at[kind]).wait_recv()

        part = pl.ds(place(c), step)
        lat_ref[part, :] = (
            resid_ref[part, :]
            + rb_ref[0, part, :].astype(F32)
            + rb_ref[1, part, :].astype(F32)
            + rb_ref[2, part, :].astype(F32)
        ).astype(BF)

    order = tuple(reversed(range(chunks)))
    xit = xi_ref[...].T
    grad_shared = mm(x_ref[...].T, dq_ref[...]) + mm(xit, dk_ref[...].astype(BF))
    grad_values = mm(xit, dv_ref[...].astype(BF))
    half = width // 2
    for s in range(2):
        projections.w[0, s] = grad_shared[s * half : (s + 1) * half]
        projections.w[1, s] = grad_values[s * half : (s + 1) * half]
    projections.begin()
    ph_ref[...] = project(
        pl.multiple_of(jnp.where(r == 0, 2 * (tokens + rim), 0), 2 * step)
    ).astype(BF)
    part_copy = link(2, ph_ref, pg_ref, partner)
    part_copy.start()
    hand_out(order[0])
    projections.send_cross()
    for c in order[1:-1]:
        hand_out(c)
    part_copy.wait()
    hand_out(0)
    weights.send_totals()
    merge(order[0])
    projections.send_pieces()
    for c in order[1:-1]:
        merge(c)
    projections.send_totals()
    merge(0)
    weights.send_back()
    resid_ref[...] = resid_ref[...] + mm(dq_ref[...], sp_ref[...], 1, 1)
    context = residual_ref[...]
    for t in range(3):
        context = context + mm(hx_ref[t * COLS : t * COLS + tokens, :], taps_ref[t])
    coded_ref[...] = (context * gain).astype(BF)
    coded_save = pltpu.make_async_copy(coded_ref, coded_hbm, local_sems.at[7])
    coded_save.start()
    projections.send_back()
    weights.send_other()
    collect(order[0])
    projections.send_other()
    for c in order[1:]:
        collect(c)
    lat_save = pltpu.make_async_copy(lat_ref, lat_hbm, local_sems.at[8])
    lat_save.start()
    weights.finish()
    projections.finish()

    passed = (hi2, lo2, always, lo2 & hi2, lo2 & hi2, relay)
    for kind in range(KINDS):

        @pl.when(passed[kind])
        def _():
            for c in range(chunks):
                copy(kind, c, x_ref, across).wait_send()

        @pl.when(sent[kind])
        def _():
            for c in range(chunks):
                give(kind, c, out_ref.at[kind]).wait_send()

    coded_save.wait()
    lat_save.wait()


def sum_scratch(size, width, n):
    dma = pltpu.SemaphoreType.DMA
    return [
        pltpu.VMEM((2, 2, size, width), F32),
        pltpu.VMEM((2, size, width), F32),
        pltpu.VMEM((size, width), BF),
        pltpu.VMEM((size, width), BF),
        pltpu.VMEM((n, size // n, width), F32),
        pltpu.VMEM((n, size // n, width), BF),
        pltpu.VMEM((n, size // n, width), BF),
        dma((10,)), dma((n,)), dma((n,)), dma((n,)), dma((n,)),
    ]


def scale_kernel(
    norm, coded_ref, lat_ref, wsum_ref, psum_ref, coded_out, lat_out, gs_ref, gv_ref, go_ref, gt_ref
):
    coded_out[...] = coded_ref[...]
    lat_out[...] = lat_ref[...]
    pieces, size = wsum_ref.shape[2:4]
    short = psum_ref.shape[3]
    for j in range(pieces):
        at = slice(j * size, (j + 1) * size)
        go_ref[at, :] = wsum_ref[0, 0, j].astype(F32) * norm
        for t in range(3):
            gt_ref[t, at, :] = wsum_ref[(t + 1) // 2, (t + 1) % 2, j].astype(F32) * norm
        for side in range(2):
            first = (side * pieces + j) * short
            at = slice(first, first + short)
            gs_ref[at, :] = psum_ref[0, side, j].astype(F32) * norm
            gv_ref[at, :] = psum_ref[1, side, j].astype(F32) * norm


def local(
    latents, ref_frames, windows, quant_level, quant_scale,
    shared_proj, value_proj, output_proj, conv_taps, cotangent,
):
    tokens, width = latents.shape[1:]
    frames = lax.axis_size("frame")
    rows = tokens // COLS
    ext = tokens + 2 * WMAX * COLS
    keys = 2 * (2 * WMAX + 1) * COLS
    wide = HALF * COLS
    rim = WMAX * COLS
    chunks = tokens // rim
    vm = pl.BlockSpec(memory_space=pltpu.VMEM)
    sm = pl.BlockSpec(memory_space=pltpu.SMEM)
    hbm = pl.BlockSpec(memory_space=pltpu.MemorySpace.HBM)
    dma = pltpu.SemaphoreType.DMA
    slab = jax.ShapeDtypeStruct((tokens, width), BF)
    square = jax.ShapeDtypeStruct((width, width), F32)
    pairs = frames // 2

    def rows_of(count, kind=BF):
        return pltpu.VMEM((count, width), kind)

    coded, grad_latents, weight_sum, projection_sum = pl.pallas_call(
        functools.partial(codec_kernel, frames),
        out_shape=(
            slab, slab,
            jax.ShapeDtypeStruct((2, 2, pairs, width // pairs, width), BF),
            jax.ShapeDtypeStruct((2, 2, pairs, width // (2 * pairs), width), BF),
        ),
        in_specs=[sm] * 3 + [hbm] * 7,
        out_specs=(hbm, hbm, vm, vm),
        scratch_shapes=[
            rows_of(tokens), rows_of(tokens), pltpu.VMEM(quant_scale.shape, F32),
            rows_of(width), rows_of(width), rows_of(width),
            pltpu.VMEM(conv_taps.shape, BF), rows_of(tokens), rows_of(tokens),
            pltpu.VMEM((KINDS, tokens, width), BF),
            pltpu.VMEM((KINDS, rim, width), BF),
            rows_of(tokens), rows_of(tokens), rows_of(tokens + 4 * COLS), rows_of(tokens, F32),
            rows_of(COLS), rows_of(tokens + 2 * COLS),
            rows_of(2 * ext), rows_of(2 * ext), rows_of(2 * ext),
            pltpu.VMEM((width, 2 * ext), BF),
            pltpu.VMEM((width, 2 * ext), BF),
            rows_of(tokens), rows_of(tokens), rows_of(2 * ext, F32), rows_of(2 * ext, F32),
            pltpu.VMEM((rows, 2, keys, wide), F32),
            pltpu.VMEM((rows, 2, keys, wide), BF),
            pltpu.VMEM((rows, 2, 1, wide), F32),
            pltpu.VMEM((RING, 2, keys, wide), F32),
            pltpu.VMEM((RING, 2, keys, wide), BF),
            pltpu.VMEM((rows, 2, wide, HALF * DH), BF),
            pltpu.VMEM((rows, 2, wide, HALF * DH), BF),
            rows_of(tokens, F32), rows_of(tokens + 2 * COLS), rows_of(COLS),
            rows_of(2 * rim), rows_of(2 * rim),
            pltpu.VMEM((KINDS, tokens, width), BF),
            pltpu.VMEM((KINDS, tokens, width), BF),
            pltpu.VMEM((2, tokens, width), BF),
            dma((KINDS, chunks)), dma((KINDS, chunks)), dma((KINDS,)), dma((KINDS,)),
            dma((KINDS, chunks)), dma((KINDS, chunks)), dma((6,)), dma((9,)),
        ]
        + sum_scratch(width, width, frames // 2)
        + sum_scratch(width // 2, width, frames // 2),
        compiler_params=pltpu.CompilerParams(
            collective_id=0, has_side_effects=True, vmem_limit_bytes=64_000_000
        ),
        name="codec",
    )(
        ref_frames, windows, quant_level, latents[0], cotangent[0], quant_scale,
        shared_proj, value_proj, output_proj, conv_taps,
    )
    total = frames * lax.axis_size("row") * tokens
    coded, grad_latents, grad_shared, grad_values, grad_output, grad_taps = pl.pallas_call(
        functools.partial(scale_kernel, 1.0 / math.sqrt(total)),
        out_shape=(
            slab, slab, square, square, square, jax.ShapeDtypeStruct((3, width, width), F32),
        ),
        in_specs=[vm] * 4,
        out_specs=(vm,) * 6,
        name="scale",
    )(coded, grad_latents, weight_sum, projection_sum)
    return (
        coded[None], grad_latents[None], grad_shared, grad_values, grad_output, grad_taps
    )


def solution(mesh):
    tok = P(("groups", "frame"), "row", None)
    frm = P(("groups", "frame"))
    placed = (tok, P(("groups", "frame"), None), frm, frm, P(), P(), P(), P(), P(), tok)
    return jax.shard_map(
        local,
        mesh=mesh,
        in_specs=placed,
        out_specs=(
            tok, tok, P("groups", None), P("groups", None), P("groups", None),
            P("groups", None, None),
        ),
        check_vma=False,
    )
```

```python
import functools
import math

import jax
import jax.numpy as jnp
from jax import lax
from jax.experimental import pallas as pl
from jax.experimental.pallas import tpu as pltpu
from jax.sharding import PartitionSpec as P

HEADS = 8
DH = 32
COLS = 64
WMAX = 2
RING = 3
LANES = 1
KINDS = 6

SCORE_SCALE = 1.5 / math.sqrt(DH)
LOG2E = math.log2(math.e)
BF = jnp.bfloat16
F32 = jnp.float32
MESH = pl.DeviceIdType.MESH


def mm(a, b, ca=1, cb=0):
    return lax.dot_general(a, b, (((ca,), (cb,)), ((), ())), preferred_element_type=F32)


HALF = 4


def masked_rows(block, f0):
    lane = lax.broadcasted_iota(jnp.int32, (1, HALF * DH), 1) // DH
    part = block[:, f0 : f0 + HALF * DH]
    return jnp.concatenate(
        [jnp.where(lane == h, part, jnp.zeros_like(part)) for h in range(HALF)], axis=0
    )


def head_diagonal(wide):
    rows = wide.T
    lane = lax.broadcasted_iota(jnp.int32, (1, HALF * DH), 1) // DH
    out = rows[:COLS]
    for h in range(1, HALF):
        out = jnp.where(lane == h, rows[h * COLS : (h + 1) * COLS], out)
    return out


def window_of(i):
    band = 2 * COLS
    skip = max(0, WMAX - i)
    first = (i + skip) * band
    return skip, first, (i + 2 * WMAX + 1) * band - first


def features(hf):
    return slice(hf * HALF * DH, (hf + 1) * HALF * DH)


def forward_row(i, bias, k_ref, qm_ref, p_ref, pb_ref, inv_ref):
    band = 2 * COLS
    wide = HALF * COLS
    skip, first, size = window_of(i)
    kk = SCORE_SCALE * LOG2E
    for hf in range(2):
        p_ref[i, hf, :size, :] = mm(k_ref[first : first + size, features(hf)], qm_ref[i, hf], 1, 1)
        m8 = None
        for c in range(size // band):
            x = p_ref[i, hf, c * band : (c + 1) * band, :].reshape(band // 8, 8, wide)
            top = jnp.max(x, axis=0) + bias[skip + c]
            m8 = top if m8 is None else jnp.maximum(m8, top)
        m = jnp.max(m8, axis=0, keepdims=True)
        l8 = jnp.zeros((8, wide), F32)
        for c in range(size // band):
            sl = slice(c * band, (c + 1) * band)
            p = jnp.exp2(p_ref[i, hf, sl, :] * kk + (bias[skip + c] - m) * kk)
            p_ref[i, hf, sl, :] = p
            l8 = l8 + jnp.sum(p.reshape(band // 8, 8, wide), axis=0)
        inv = 1.0 / jnp.sum(l8, axis=0, keepdims=True)
        inv_ref[i, hf] = inv
        for c in range(size // band):
            sl = slice(c * band, (c + 1) * band)
            pb_ref[i, hf, sl, :] = (p_ref[i, hf, sl, :] * inv).astype(BF)


def mix_row(i, at, vt_ref, pb_ref, mix_ref):
    _, first, size = window_of(i)
    for hf in range(2):
        ft = features(hf)
        mix = mm(vt_ref[ft, first : first + size], pb_ref[i, hf, :size, :])
        mix_ref[pl.ds(at, COLS), ft] = head_diagonal(mix).astype(BF)


def score_row(i, v_ref, dom_ref, p_ref, inv_ref, dp_ref, ds_ref):
    band = 2 * COLS
    wide = HALF * COLS
    slot = i % RING
    _, first, size = window_of(i)
    for hf in range(2):
        dp_ref[slot, hf, :size, :] = mm(
            v_ref[first : first + size, features(hf)], dom_ref[i, hf], 1, 1
        )
        u8 = jnp.zeros((8, wide), F32)
        for c in range(size // band):
            sl = slice(c * band, (c + 1) * band)
            x = p_ref[i, hf, sl, :] * dp_ref[slot, hf, sl, :]
            u8 = u8 + jnp.sum(x.reshape(band // 8, 8, wide), axis=0)
        inv = inv_ref[i, hf]
        ci = inv * SCORE_SCALE
        inner = jnp.sum(u8, axis=0, keepdims=True) * inv * ci
        for c in range(size // band):
            sl = slice(c * band, (c + 1) * band)
            ds_ref[slot, hf, sl, :] = (
                p_ref[i, hf, sl, :] * (dp_ref[slot, hf, sl, :] * ci - inner)
            ).astype(BF)


def query_row(i, at, kt_ref, ds_ref, dq_ref):
    _, first, size = window_of(i)
    for hf in range(2):
        ft = features(hf)
        dq = mm(kt_ref[ft, first : first + size], ds_ref[i % RING, hf, :size, :])
        dq_ref[pl.ds(at, COLS), ft] = head_diagonal(dq).astype(BF)


def key_row(i, qm_ref, dom_ref, pb_ref, ds_ref, dk_ref, dv_ref):
    _, first, size = window_of(i)
    win = slice(first, first + size)
    for hf in range(2):
        ft = features(hf)
        dk_ref[win, ft] += mm(ds_ref[i % RING, hf, :size, :], qm_ref[i, hf])
        dv_ref[win, ft] += mm(pb_ref[i, hf, :size, :], dom_ref[i, hf])


def loop(first, last, body):
    lax.fori_loop(first, last, lambda k, carry: (body(k), carry)[1], 0)


class Sum:
    def __init__(self, refs, res, f, r, frames):
        (self.w, self.p, self.xs, self.xr, self.zw, self.zs, self.zr,
         self.one, self.zss, self.zsr, self.gs, self.gr) = refs
        self.res = res
        self.n = frames // 2
        self.r, self.odd, self.me = r, lax.rem(f, 2), f // 2
        self.across = {"frame": f + 1 - 2 * self.odd}
        self.partner = {"row": 1 - r}

    def link(self, i, source, target, device):
        return pltpu.make_async_remote_copy(
            source, target, self.one.at[2 * i], self.one.at[2 * i + 1],
            device_id=device, device_id_type=MESH,
        )

    def pair(self):
        return self.link(0, self.w.at[1 - self.r], self.p, self.partner)

    def cross(self):
        return self.link(1, self.xs, self.xr, self.across)

    def cross_back(self):
        part = self.res.at[self.r, self.odd]
        return self.link(2, part, part, self.across)

    def pair_back(self, i):
        side = self.odd if i == 0 else 1 - self.odd
        part = self.res.at[self.r, side]
        return self.link(3 + i, part, part, self.partner)

    def scatter(self, k, incoming):
        other = lax.rem(self.me + k, self.n)
        if incoming:
            return pltpu.make_async_remote_copy(
                self.zs.at[other], self.zr.at[other], self.zss.at[k], self.zsr.at[other],
                device_id={"frame": 2 * other + self.odd}, device_id_type=MESH,
            )
        return pltpu.make_async_remote_copy(
            self.zs.at[other], self.zr.at[self.me], self.zss.at[k], self.zsr.at[self.me],
            device_id={"frame": 2 * other + self.odd}, device_id_type=MESH,
        )

    def gather(self, k, incoming):
        other = lax.rem(self.me + k, self.n)
        slot = other if incoming else self.me
        part = self.res.at[self.r, self.odd, slot]
        return pltpu.make_async_remote_copy(
            part, part, self.gs.at[k], self.gr.at[slot],
            device_id={"frame": 2 * other + self.odd}, device_id_type=MESH,
        )

    def begin(self):
        self.pair().start()

    def send_cross(self):
        self.pair().wait()
        away = 1 - self.odd
        self.xs[...] = (self.w[self.r, away] + self.p[away]).astype(BF)
        self.cross().start()

    def send_pieces(self):
        self.cross().wait()
        total = self.w[self.r, self.odd] + self.p[self.odd] + self.xr[...].astype(F32)
        size = total.shape[0] // self.n
        for j in range(self.n):
            piece = total[j * size : (j + 1) * size]
            self.zw[j] = piece
            self.zs[j] = piece.astype(BF)
        loop(1, self.n, lambda k: self.scatter(k, False).start())

    def send_totals(self):
        def add(k, total):
            self.scatter(k, True).wait_recv()
            return total + self.zr[lax.rem(self.me + k, self.n)].astype(F32)

        total = lax.fori_loop(1, self.n, add, self.zw[self.me])
        self.res[self.r, self.odd, self.me] = total.astype(BF)
        loop(1, self.n, lambda k: self.gather(k, False).start())

    def send_back(self):
        loop(1, self.n, lambda k: self.gather(k, True).wait_recv())
        self.cross_back().start()
        self.pair_back(0).start()

    def send_other(self):
        self.cross_back().wait_recv()
        self.pair_back(1).start()

    def finish(self):
        self.pair_back(0).wait()
        self.pair_back(1).wait()
        self.cross_back().wait_send()

        def sent(k):
            self.scatter(k, False).wait_send()
            self.gather(k, False).wait_send()

        loop(1, self.n, sent)

def codec_kernel(
    frames, refs_ref, window_ref, level_ref, *rest,
):
    inputs, rest = rest[:7], rest[7:]
    (coded_hbm, lat_hbm), totals, rest = rest[:2], rest[2 : 2 + 2 * LANES], rest[2 + 2 * LANES :]
    held, rest = rest[:9], rest[9:]
    x_ref, ct_ref, qs_ref, sp_ref, vp_ref, op_ref, taps_ref, coded_ref, lat_ref = held
    chunks = x_ref.shape[0] // (WMAX * COLS)
    buf_refs, rest = rest[:chunks], rest[chunks:]
    (
        halo_ref, q_ref, do_ref, gp_ref, resid_ref, cth_ref, ext_ref, xi_ref, k_ref,
        v_ref, kt_ref, vt_ref, mix_ref, dq_ref, dk_ref, dv_ref, p_ref, pb_ref, inv_ref, dp_ref,
        ds_ref, qm_ref, dom_ref, residual_ref, hx_ref, eh_ref, ph_ref, pg_ref, edge_ref, out_ref, rb_ref,
        sb_ref, ssem, rsem, hs, hr, bs, br, one, local_sems,
    ), sums = rest[:40], rest[40:]
    f = lax.axis_index("frame")
    r = lax.axis_index("row")
    tokens, width = x_ref.shape
    rows = tokens // COLS
    rim = WMAX * COLS
    step = rim

    def row_at(i):
        return pl.multiple_of(jnp.where(r == 0, i, rows - 1 - i) * COLS, COLS)

    odd = lax.rem(f, 2)
    pair = f + 1 - 2 * odd
    lo2, hi2, lo4, hi4 = f >= 2, f + 2 < frames, f >= 4, f + 4 < frames
    side = ((odd == 1) & (f + 1 < frames)) | ((odd == 0) & (f >= 1))
    relay = ((odd == 1) & lo2) | ((odd == 0) & hi2)
    always = f >= 0
    partner = {"row": 1 - r}
    up, down, across = {"frame": f + 2}, {"frame": f - 2}, {"frame": pair}
    lanes = [
        Sum(sums[12 * i : 12 * i + 12], totals[i], f, r, frames) for i in range(2 * LANES)
    ]
    weights, projections = lanes[:LANES], lanes[LANES:]

    loads = [
        pltpu.make_async_copy(source, target, local_sems.at[i])
        for i, (source, target) in enumerate(zip(inputs, held))
    ]
    for load in loads:
        load.start()
    barrier = pltpu.get_barrier_semaphore()
    pl.semaphore_signal(barrier, inc=1, device_id=partner, device_id_type=MESH)
    pl.semaphore_signal(barrier, inc=1, device_id=across, device_id_type=MESH)

    def hello(k):
        other = {"frame": lax.rem(f + 2 * k, frames)}
        pl.semaphore_signal(barrier, inc=1, device_id=other, device_id_type=MESH)

    loop(1, frames // 2, hello)
    pl.semaphore_wait(barrier, frames // 2 + 1)

    def link(i, source, target, device):
        return pltpu.make_async_remote_copy(
            source, target, one.at[2 * i], one.at[2 * i + 1],
            device_id=device, device_id_type=MESH,
        )

    def place(c):
        return pl.multiple_of(jnp.where(r == 0, chunks - 1 - c, c) * step, step)

    loads[0].wait()
    edge = pl.multiple_of((1 - r) * (tokens - COLS), COLS)

    def copy(kind, c, source, device):
        if source is x_ref:
            source = x_ref.at[pl.ds(place(c), step)]
        return pltpu.make_async_remote_copy(
            source, buf_refs[c].at[kind], ssem.at[kind, c], rsem.at[kind, c],
            device_id=device, device_id_type=MESH,
        )

    def halo(kind):
        return pltpu.make_async_remote_copy(
            buf_refs[0].at[kind], halo_ref.at[kind], hs.at[kind], hr.at[kind],
            device_id=partner, device_id_type=MESH,
        )

    have = (lo2, hi2, always, lo4, hi4, side)
    hops = ((0, hi2, up), (1, lo2, down), (2, always, across))

    def launch(c):
        for kind, exists, target in hops:

            @pl.when(exists)
            def _():
                copy(kind, c, x_ref, target).start()

    def launched(c):
        for kind, exists, target in hops:

            @pl.when(exists)
            def _():
                copy(kind, c, x_ref, target).wait_send()

    launch(0)
    launch(1)
    for load in loads[1:]:
        load.wait()
    ct_copy = link(0, ct_ref.at[pl.ds(edge, COLS)], cth_ref, partner)
    ct_copy.start()

    def pass_on(c):
        @pl.when(lo2)
        def _():
            copy(0, c, x_ref, across).wait_recv()
            if c == 0:
                halo(0).start()

        @pl.when(lo2 & hi2)
        def _():
            copy(3, c, buf_refs[c].at[0], up).start()

        @pl.when(lo2 & (odd == 1))
        def _():
            copy(5, c, buf_refs[c].at[0], across).start()

        @pl.when(hi2)
        def _():
            copy(1, c, x_ref, across).wait_recv()
            if c == 0:
                halo(1).start()

        @pl.when(hi2 & lo2)
        def _():
            copy(4, c, buf_refs[c].at[1], down).start()

        @pl.when(hi2 & (odd == 0))
        def _():
            copy(5, c, buf_refs[c].at[1], across).start()

    level = lax.broadcasted_iota(jnp.int32, (qs_ref.shape[0], 1), 0)
    gain = jnp.sum(
        jnp.where(level == level_ref[0], qs_ref[...], 0.0), axis=0, keepdims=True
    )
    q_ref[...] = mm(x_ref[...], sp_ref[...]).astype(BF)
    grad_z = ct_ref[...].astype(F32) * gain
    resid_ref[...] = grad_z
    grad_zb = grad_z.astype(BF)
    gp_ref[: 2 * COLS, :] = jnp.zeros((2 * COLS, width), BF)
    gp_ref[2 * COLS : 2 * COLS + tokens, :] = grad_zb
    gp_ref[2 * COLS + tokens :, :] = jnp.zeros((2 * COLS, width), BF)
    ext_ref[COLS : COLS + tokens, :] = grad_zb
    dk_ref[...] = jnp.zeros_like(dk_ref)
    dv_ref[...] = jnp.zeros_like(dv_ref)
    got = (lo2, hi2, always, lo2 & hi2, lo2 & hi2, relay)
    for kind in (0, 1, 3, 4, 5):

        @pl.when(jnp.logical_not(got[kind]))
        def _():
            rb_ref[kind, :, :] = jnp.zeros((tokens, width), BF)

    launched(0)
    launch(2)
    ct_copy.wait()
    outer = (cth_ref[...].astype(F32) * gain).astype(BF)
    blank = jnp.zeros_like(outer)
    ext_ref[:COLS, :] = jnp.where(r == 0, blank, outer)
    ext_ref[COLS + tokens :, :] = jnp.where(r == 0, outer, blank)
    pass_on(0)
    for c in range(3, chunks):
        launched(c - 2)
        launch(c)
    resid = resid_ref[...]
    for t in range(3):
        resid = resid + mm(ext_ref[(2 - t) * COLS : (2 - t) * COLS + tokens, :], taps_ref[t], 1, 1)
    resid_ref[...] = resid
    pass_on(1)
    do_ref[...] = mm(resid_ref[...].astype(BF), op_ref[...], 1, 1).astype(BF)
    copy(2, 0, x_ref, across).wait_recv()
    halo(2).start()
    for c in range(max(0, chunks - 2), chunks):
        launched(c)
    for c in range(2, chunks):
        pass_on(c)
    for i in range(rows):
        tok = pl.ds(row_at(i), COLS)
        query, grad = q_ref[tok, :], do_ref[tok, :]
        for hf in range(2):
            qm_ref[i, hf] = masked_rows(query, hf * HALF * DH)
            dom_ref[i, hf] = masked_rows(grad, hf * HALF * DH)
    sources = (f - 2, f + 2, pair, f - 4, f + 4, f - 1 + 2 * odd)
    targets = (f + 2, f - 2, pair, f + 4, f - 4, f - 1 + 2 * odd)
    kinds = []
    for s in range(2):
        own = refs_ref[0, s]
        kind = jnp.int32(0)
        for number, source in enumerate(sources):
            kind = jnp.where(own == source, number, kind)
        kinds.append(kind)

    def arrive(c):
        for kind in range(2, KINDS):
            if kind > 2 or c:

                @pl.when(have[kind])
                def _():
                    copy(kind, c, x_ref, across).wait_recv()
                    if c == 0:
                        halo(kind).start()

    def take(first, piece):
        for d in range(WMAX):
            for s in range(2):
                at = (2 * (first + d) + s) * COLS
                xi_ref[at : at + COLS, :] = piece(s, d)
        part = slice(2 * first * COLS, 2 * (first + WMAX) * COLS)
        keys = mm(xi_ref[part, :], sp_ref[...]).astype(BF)
        k_ref[part, :] = keys
        kt_ref[:, part] = keys.T
        vals = mm(xi_ref[part, :], vp_ref[...]).astype(BF)
        v_ref[part, :] = vals
        vt_ref[:, part] = vals.T

    def sub(d):
        return pl.ds(pl.multiple_of(jnp.where(r == 0, d, 1 - d) * COLS, COLS), COLS)

    def take_chunk(c):
        take(WMAX + rows - WMAX * (c + 1), lambda s, d: buf_refs[c][kinds[s], sub(d), :])

    window = window_ref[0]
    bias = [
        jnp.where(abs(c - WMAX) <= window, 0.0, -jnp.inf).astype(F32) for c in range(2 * WMAX + 1)
    ]

    def forward(last, first):
        for i in range(last, first - 1, -1):
            forward_row(i, bias, k_ref, qm_ref, p_ref, pb_ref, inv_ref)

    def mix(last, first):
        for i in range(last, first - 1, -1):
            mix_row(i, row_at(i), vt_ref, pb_ref, mix_ref)

    arrive(0)
    arrive(1)
    take_chunk(0)
    take_chunk(1)
    for kind in range(KINDS):

        @pl.when(have[kind])
        def _():
            halo(kind).wait()

    take(WMAX + rows, lambda s, d: halo_ref[kinds[s], sub(d), :])
    low = rows - WMAX
    forward(rows - 1, low)
    mix(rows - 1, low)
    inner = row_at(rows - 1)
    edge_ref[...] = (
        x_ref[pl.ds(inner, COLS), :].astype(F32) + mm(mix_ref[pl.ds(inner, COLS), :], op_ref[...])
    ).astype(BF)
    hidden_copy = link(1, edge_ref, eh_ref, partner)
    hidden_copy.start()
    for c in range(2, chunks):
        arrive(c)
        take_chunk(c)
        below = low - WMAX if c < chunks - 1 else 0
        forward(low - 1, below)
        mix(low - 1, below)
        low = below

    residual = x_ref[...].astype(F32) + mm(mix_ref[...], op_ref[...])
    residual_ref[...] = residual
    hx_ref[COLS : COLS + tokens, :] = residual.astype(BF)

    def fill(half, side, value):
        size = width // LANES
        for i, lane in enumerate(weights):
            lane.w[half, side] = value[i * size : (i + 1) * size]

    fill(0, 0, mm(mix_ref[...].T, resid_ref[...].astype(BF)))
    hidden_copy.wait()
    outer = eh_ref[...]
    blank = jnp.zeros_like(outer)
    hx_ref[:COLS, :] = jnp.where(r == 0, blank, outer)
    hx_ref[COLS + tokens :, :] = jnp.where(r == 0, outer, blank)
    hxt = hx_ref[...].T
    span = tokens + 2 * COLS
    for t in range(3):
        fill((t + 1) // 2, (t + 1) % 2, mm(hxt, gp_ref[(2 - t) * COLS : (2 - t) * COLS + span, :]))
    for lane in weights:
        lane.begin()

    def project(first):
        part = slice(2 * first * COLS, 2 * (first + WMAX) * COLS)
        return mm(dk_ref[part, :].astype(BF), sp_ref[...], 1, 1) + mm(
            dv_ref[part, :].astype(BF), vp_ref[...], 1, 1
        )

    part_copy = link(2, ph_ref, pg_ref, partner)
    sent = (hi2, lo2, always, hi4, lo4, side)
    device = (up, down, across, up, down, across)

    def give(kind, c, source):
        part = pl.ds(place(c), step)
        return pltpu.make_async_remote_copy(
            source.at[part], rb_ref.at[kind, part], bs.at[kind, c], br.at[kind, c],
            device_id=device[kind], device_id_type=MESH,
        )

    def hand_out(c):
        first = rows - WMAX * (c + 1)
        block = project(WMAX + first)
        if c == 0:
            band = 2 * COLS
            block = block + jnp.concatenate([pg_ref[band:, :], pg_ref[:band, :]], axis=0).astype(F32)
        for kind, target in enumerate(targets):
            one_is = refs_ref[0, 0] == target
            two_is = refs_ref[0, 1] == target
            for d in range(WMAX):
                part = jnp.where(one_is, block[2 * d * COLS : (2 * d + 1) * COLS], 0.0)
                part = part + jnp.where(two_is, block[(2 * d + 1) * COLS : (2 * d + 2) * COLS], 0.0)
                out_ref[kind, pl.ds(row_at(first + d), COLS), :] = part.astype(BF)
        for kind in (3, 4, 5):

            @pl.when(sent[kind])
            def _():
                give(kind, c, out_ref.at[kind]).start()

    even = jnp.where(odd == 0, 1.0, 0.0).astype(F32)

    def merge(c):
        for kind in (3, 4, 5):

            @pl.when(got[kind])
            def _():
                give(kind, c, out_ref.at[kind]).wait_recv()

        give(2, c, out_ref.at[2]).start()
        part = pl.ds(place(c), step)
        extra = rb_ref[5, part, :].astype(F32)
        rising = out_ref[0, part, :].astype(F32) + rb_ref[3, part, :].astype(F32) + extra * even
        falling = (
            out_ref[1, part, :].astype(F32) + rb_ref[4, part, :].astype(F32) + extra * (1.0 - even)
        )
        sb_ref[0, part, :] = rising.astype(BF)
        sb_ref[1, part, :] = falling.astype(BF)

        @pl.when(hi2)
        def _():
            give(0, c, sb_ref.at[0]).start()

        @pl.when(lo2)
        def _():
            give(1, c, sb_ref.at[1]).start()

    def collect(c):
        for kind in (0, 1, 2):

            @pl.when(got[kind])
            def _():
                give(kind, c, out_ref.at[kind]).wait_recv()

        part = pl.ds(place(c), step)
        lat_ref[part, :] = (
            resid_ref[part, :]
            + rb_ref[0, part, :].astype(F32)
            + rb_ref[1, part, :].astype(F32)
            + rb_ref[2, part, :].astype(F32)
        ).astype(BF)

    for t in range(rows + 1):
        i = rows - 1 - t
        if t == 2:
            for lane in weights:
                lane.send_cross()
        if t > rows - 3 and t - (rows - 2) < LANES:
            weights[t - (rows - 2)].send_pieces()
        if t < rows:
            score_row(i, v_ref, dom_ref, p_ref, inv_ref, dp_ref, ds_ref)
        if t:
            key_row(i + 1, qm_ref, dom_ref, pb_ref, ds_ref, dk_ref, dv_ref)
            query_row(i + 1, row_at(i + 1), kt_ref, ds_ref, dq_ref)
        if t == WMAX:
            ph_ref[...] = project(WMAX + rows).astype(BF)
            part_copy.start()
        if t == 2 * WMAX:
            part_copy.wait()
            hand_out(0)
        if t > 2 * WMAX and t % WMAX == 0 and t < rows:
            hand_out(t // WMAX - WMAX)
    inside = 2 * WMAX * COLS
    xit = xi_ref[inside:, :].T
    grad_shared = mm(x_ref[...].T, dq_ref[...]) + mm(xit, dk_ref[inside:, :].astype(BF))
    grad_values = mm(xit, dv_ref[inside:, :].astype(BF))
    short = width // (2 * LANES)
    for i, lane in enumerate(projections):
        for side_ in range(2):
            part = slice((2 * i + side_) * short, (2 * i + side_ + 1) * short)
            lane.w[0, side_] = grad_shared[part]
            lane.w[1, side_] = grad_values[part]
        lane.begin()
    hand_out(2)
    hand_out(3)
    for lane in projections:
        lane.send_cross()
    for lane in weights:
        lane.send_totals()
    for lane in projections:
        lane.send_pieces()
    merge(0)
    merge(1)
    for lane in projections:
        lane.send_totals()
    for lane in weights:
        lane.send_back()
    merge(2)
    merge(3)
    for lane in projections:
        lane.send_back()
    for lane in weights:
        lane.send_other()
    resid_ref[...] = resid_ref[...] + mm(dq_ref[...], sp_ref[...], 1, 1)
    context = residual_ref[...]
    for t in range(3):
        context = context + mm(hx_ref[t * COLS : t * COLS + tokens, :], taps_ref[t])
    coded_ref[...] = (context * gain).astype(BF)
    coded_save = pltpu.make_async_copy(coded_ref, coded_hbm, local_sems.at[7])
    coded_save.start()
    for lane in projections:
        lane.send_other()
    collect(0)
    collect(1)
    collect(2)
    collect(3)
    lat_save = pltpu.make_async_copy(lat_ref, lat_hbm, local_sems.at[8])
    lat_save.start()
    for lane in lanes:
        lane.finish()

    for kind in range(KINDS):

        if kind > 2:

            @pl.when(got[kind])
            def _():
                for c in range(chunks):
                    copy(kind, c, x_ref, across).wait_send()

        @pl.when(sent[kind])
        def _():
            for c in range(chunks):
                give(kind, c, out_ref.at[kind]).wait_send()

    coded_save.wait()
    lat_save.wait()


def sum_scratch(size, width, n):
    dma = pltpu.SemaphoreType.DMA
    return [
        pltpu.VMEM((2, 2, size, width), F32),
        pltpu.VMEM((2, size, width), F32),
        pltpu.VMEM((size, width), BF),
        pltpu.VMEM((size, width), BF),
        pltpu.VMEM((n, size // n, width), F32),
        pltpu.VMEM((n, size // n, width), BF),
        pltpu.VMEM((n, size // n, width), BF),
        dma((10,)), dma((n,)), dma((n,)), dma((n,)), dma((n,)),
    ]


def scale_kernel(norm, coded_ref, lat_ref, *rest):
    totals = rest[: 2 * LANES]
    coded_out, lat_out, gs_ref, gv_ref, go_ref, gt_ref = rest[2 * LANES :]
    coded_out[...] = coded_ref[...]
    lat_out[...] = lat_ref[...]
    for i in range(LANES):
        large, small = totals[i], totals[LANES + i]
        pieces, size = large.shape[2:4]
        short = small.shape[3]
        for j in range(pieces):
            at = pl.ds((i * pieces + j) * size, size)
            go_ref[at, :] = large[0, 0, j].astype(F32) * norm
            for t in range(3):
                gt_ref[t, at, :] = large[(t + 1) // 2, (t + 1) % 2, j].astype(F32) * norm
            for side in range(2):
                at = pl.ds(((2 * i + side) * pieces + j) * short, short)
                gs_ref[at, :] = small[0, side, j].astype(F32) * norm
                gv_ref[at, :] = small[1, side, j].astype(F32) * norm


def local(
    latents, ref_frames, windows, quant_level, quant_scale,
    shared_proj, value_proj, output_proj, conv_taps, cotangent,
):
    tokens, width = latents.shape[1:]
    frames = lax.axis_size("frame")
    rows = tokens // COLS
    ext = tokens + 2 * WMAX * COLS
    keys = 2 * (2 * WMAX + 1) * COLS
    wide = HALF * COLS
    rim = WMAX * COLS
    chunks = tokens // rim
    vm = pl.BlockSpec(memory_space=pltpu.VMEM)
    sm = pl.BlockSpec(memory_space=pltpu.SMEM)
    hbm = pl.BlockSpec(memory_space=pltpu.MemorySpace.HBM)
    dma = pltpu.SemaphoreType.DMA
    slab = jax.ShapeDtypeStruct((tokens, width), BF)
    square = jax.ShapeDtypeStruct((width, width), F32)
    pairs = frames // 2
    sizes = (width // LANES,) * LANES + (width // (2 * LANES),) * LANES

    def rows_of(count, kind=BF):
        return pltpu.VMEM((count, width), kind)

    coded, grad_latents, *totals = pl.pallas_call(
        functools.partial(codec_kernel, frames),
        out_shape=(
            slab, slab,
        )
        + tuple(
            jax.ShapeDtypeStruct((2, 2, pairs, size // pairs, width), BF) for size in sizes
        ),
        in_specs=[sm] * 3 + [hbm] * 7,
        out_specs=(hbm, hbm) + (vm,) * (2 * LANES),
        scratch_shapes=[
            rows_of(tokens), rows_of(tokens), pltpu.VMEM(quant_scale.shape, F32),
            rows_of(width), rows_of(width), rows_of(width),
            pltpu.VMEM(conv_taps.shape, BF), rows_of(tokens), rows_of(tokens),
        ]
        + [pltpu.VMEM((KINDS, rim, width), BF)] * (chunks + 1)
        + [
            rows_of(tokens), rows_of(tokens), rows_of(tokens + 4 * COLS), rows_of(tokens, F32),
            rows_of(COLS), rows_of(tokens + 2 * COLS),
            rows_of(2 * ext), rows_of(2 * ext), rows_of(2 * ext),
            pltpu.VMEM((width, 2 * ext), BF),
            pltpu.VMEM((width, 2 * ext), BF),
            rows_of(tokens), rows_of(tokens), rows_of(2 * ext, F32), rows_of(2 * ext, F32),
            pltpu.VMEM((rows, 2, keys, wide), F32),
            pltpu.VMEM((rows, 2, keys, wide), BF),
            pltpu.VMEM((rows, 2, 1, wide), F32),
            pltpu.VMEM((RING, 2, keys, wide), F32),
            pltpu.VMEM((RING, 2, keys, wide), BF),
            pltpu.VMEM((rows, 2, wide, HALF * DH), BF),
            pltpu.VMEM((rows, 2, wide, HALF * DH), BF),
            rows_of(tokens, F32), rows_of(tokens + 2 * COLS), rows_of(COLS),
            rows_of(2 * rim), rows_of(2 * rim), rows_of(COLS),
            pltpu.VMEM((KINDS, tokens, width), BF),
            pltpu.VMEM((KINDS, tokens, width), BF),
            pltpu.VMEM((2, tokens, width), BF),
            dma((KINDS, chunks)), dma((KINDS, chunks)), dma((KINDS,)), dma((KINDS,)),
            dma((KINDS, chunks)), dma((KINDS, chunks)), dma((6,)), dma((9,)),
        ]
        + [ref for size in sizes for ref in sum_scratch(size, width, pairs)],
        compiler_params=pltpu.CompilerParams(
            collective_id=0, has_side_effects=True, vmem_limit_bytes=64_000_000
        ),
        name="codec",
    )(
        ref_frames, windows, quant_level, latents[0], cotangent[0], quant_scale,
        shared_proj, value_proj, output_proj, conv_taps,
    )
    total = frames * lax.axis_size("row") * tokens
    coded, grad_latents, grad_shared, grad_values, grad_output, grad_taps = pl.pallas_call(
        functools.partial(scale_kernel, 1.0 / math.sqrt(total)),
        out_shape=(
            slab, slab, square, square, square, jax.ShapeDtypeStruct((3, width, width), F32),
        ),
        in_specs=[vm] * (2 + 2 * LANES),
        out_specs=(vm,) * 6,
        name="scale",
    )(coded, grad_latents, *totals)
    return (
        coded[None], grad_latents[None], grad_shared, grad_values, grad_output, grad_taps
    )


def solution(mesh):
    tok = P(("groups", "frame"), "row", None)
    frm = P(("groups", "frame"))
    placed = (tok, P(("groups", "frame"), None), frm, frm, P(), P(), P(), P(), P(), tok)
    return jax.shard_map(
        local,
        mesh=mesh,
        in_specs=placed,
        out_specs=(
            tok, tok, P("groups", None), P("groups", None), P("groups", None),
            P("groups", None, None),
        ),
        check_vma=False,
    )
```

```python
import functools
import math

import jax
import jax.numpy as jnp
from jax import lax
from jax.experimental import pallas as pl
from jax.experimental.pallas import tpu as pltpu
from jax.sharding import PartitionSpec as P

HEADS = 8
DH = 32
COLS = 64
WMAX = 2
RING = 3
LANES = 1
KINDS = 6

SCORE_SCALE = 1.5 / math.sqrt(DH)
LOG2E = math.log2(math.e)
BF = jnp.bfloat16
F32 = jnp.float32
MESH = pl.DeviceIdType.MESH


def mm(a, b, ca=1, cb=0):
    return lax.dot_general(a, b, (((ca,), (cb,)), ((), ())), preferred_element_type=F32)


HALF = 4


def masked_rows(block, f0):
    lane = lax.broadcasted_iota(jnp.int32, (1, HALF * DH), 1) // DH
    part = block[:, f0 : f0 + HALF * DH]
    return jnp.concatenate(
        [jnp.where(lane == h, part, jnp.zeros_like(part)) for h in range(HALF)], axis=0
    )


def head_diagonal(wide):
    rows = wide.T
    lane = lax.broadcasted_iota(jnp.int32, (1, HALF * DH), 1) // DH
    out = rows[:COLS]
    for h in range(1, HALF):
        out = jnp.where(lane == h, rows[h * COLS : (h + 1) * COLS], out)
    return out


def window_of(i):
    band = 2 * COLS
    skip = max(0, WMAX - i)
    first = (i + skip) * band
    return skip, first, (i + 2 * WMAX + 1) * band - first


def features(hf):
    return slice(hf * HALF * DH, (hf + 1) * HALF * DH)


def forward_row(i, bias, k_ref, qm_ref, p_ref, pb_ref, inv_ref):
    band = 2 * COLS
    wide = HALF * COLS
    skip, first, size = window_of(i)
    kk = SCORE_SCALE * LOG2E
    for hf in range(2):
        p_ref[i, hf, :size, :] = mm(k_ref[first : first + size, features(hf)], qm_ref[i, hf], 1, 1)
        m8 = None
        for c in range(size // band):
            x = p_ref[i, hf, c * band : (c + 1) * band, :].reshape(band // 8, 8, wide)
            top = jnp.max(x, axis=0) + bias[skip + c]
            m8 = top if m8 is None else jnp.maximum(m8, top)
        m = jnp.max(m8, axis=0, keepdims=True)
        l8 = jnp.zeros((8, wide), F32)
        for c in range(size // band):
            sl = slice(c * band, (c + 1) * band)
            p = jnp.exp2(p_ref[i, hf, sl, :] * kk + (bias[skip + c] - m) * kk)
            p_ref[i, hf, sl, :] = p
            l8 = l8 + jnp.sum(p.reshape(band // 8, 8, wide), axis=0)
        inv = 1.0 / jnp.sum(l8, axis=0, keepdims=True)
        inv_ref[i, hf] = inv
        for c in range(size // band):
            sl = slice(c * band, (c + 1) * band)
            pb_ref[i, hf, sl, :] = (p_ref[i, hf, sl, :] * inv).astype(BF)


def mix_row(i, at, vt_ref, pb_ref, mix_ref):
    _, first, size = window_of(i)
    for hf in range(2):
        ft = features(hf)
        mix = mm(vt_ref[ft, first : first + size], pb_ref[i, hf, :size, :])
        mix_ref[pl.ds(at, COLS), ft] = head_diagonal(mix).astype(BF)


def score_row(i, v_ref, dom_ref, p_ref, inv_ref, dp_ref, ds_ref):
    band = 2 * COLS
    wide = HALF * COLS
    slot = i % RING
    _, first, size = window_of(i)
    for hf in range(2):
        dp_ref[slot, hf, :size, :] = mm(
            v_ref[first : first + size, features(hf)], dom_ref[i, hf], 1, 1
        )
        u8 = jnp.zeros((8, wide), F32)
        for c in range(size // band):
            sl = slice(c * band, (c + 1) * band)
            x = p_ref[i, hf, sl, :] * dp_ref[slot, hf, sl, :]
            u8 = u8 + jnp.sum(x.reshape(band // 8, 8, wide), axis=0)
        inv = inv_ref[i, hf]
        ci = inv * SCORE_SCALE
        inner = jnp.sum(u8, axis=0, keepdims=True) * inv * ci
        for c in range(size // band):
            sl = slice(c * band, (c + 1) * band)
            ds_ref[slot, hf, sl, :] = (
                p_ref[i, hf, sl, :] * (dp_ref[slot, hf, sl, :] * ci - inner)
            ).astype(BF)


def query_row(i, at, kt_ref, ds_ref, dq_ref):
    _, first, size = window_of(i)
    for hf in range(2):
        ft = features(hf)
        dq = mm(kt_ref[ft, first : first + size], ds_ref[i % RING, hf, :size, :])
        dq_ref[pl.ds(at, COLS), ft] = head_diagonal(dq).astype(BF)


def key_row(i, qm_ref, dom_ref, pb_ref, ds_ref, dk_ref, dv_ref):
    _, first, size = window_of(i)
    win = slice(first, first + size)
    for hf in range(2):
        ft = features(hf)
        dk_ref[win, ft] += mm(ds_ref[i % RING, hf, :size, :], qm_ref[i, hf])
        dv_ref[win, ft] += mm(pb_ref[i, hf, :size, :], dom_ref[i, hf])


def loop(first, last, body):
    lax.fori_loop(first, last, lambda k, carry: (body(k), carry)[1], 0)


class Sum:
    def __init__(self, refs, res, f, r, frames):
        (self.w, self.p, self.xs, self.xr, self.zw, self.zs, self.zr,
         self.one, self.zss, self.zsr, self.gs, self.gr) = refs
        self.res = res
        self.n = frames // 2
        self.r, self.odd, self.me = r, lax.rem(f, 2), f // 2
        self.across = {"frame": f + 1 - 2 * self.odd}
        self.partner = {"row": 1 - r}

    def link(self, i, source, target, device):
        return pltpu.make_async_remote_copy(
            source, target, self.one.at[2 * i], self.one.at[2 * i + 1],
            device_id=device, device_id_type=MESH,
        )

    def pair(self):
        return self.link(0, self.w.at[1 - self.r], self.p, self.partner)

    def cross(self):
        return self.link(1, self.xs, self.xr, self.across)

    def cross_back(self):
        part = self.res.at[self.r, self.odd]
        return self.link(2, part, part, self.across)

    def pair_back(self, i):
        side = self.odd if i == 0 else 1 - self.odd
        part = self.res.at[self.r, side]
        return self.link(3 + i, part, part, self.partner)

    def scatter(self, k, incoming):
        other = lax.rem(self.me + k, self.n)
        if incoming:
            return pltpu.make_async_remote_copy(
                self.zs.at[other], self.zr.at[other], self.zss.at[k], self.zsr.at[other],
                device_id={"frame": 2 * other + self.odd}, device_id_type=MESH,
            )
        return pltpu.make_async_remote_copy(
            self.zs.at[other], self.zr.at[self.me], self.zss.at[k], self.zsr.at[self.me],
            device_id={"frame": 2 * other + self.odd}, device_id_type=MESH,
        )

    def gather(self, k, incoming):
        other = lax.rem(self.me + k, self.n)
        slot = other if incoming else self.me
        part = self.res.at[self.r, self.odd, slot]
        return pltpu.make_async_remote_copy(
            part, part, self.gs.at[k], self.gr.at[slot],
            device_id={"frame": 2 * other + self.odd}, device_id_type=MESH,
        )

    def begin(self):
        self.pair().start()

    def send_cross(self):
        self.pair().wait()
        away = 1 - self.odd
        self.xs[...] = (self.w[self.r, away] + self.p[away]).astype(BF)
        self.cross().start()

    def send_pieces(self):
        self.cross().wait()
        total = self.w[self.r, self.odd] + self.p[self.odd] + self.xr[...].astype(F32)
        size = total.shape[0] // self.n
        for j in range(self.n):
            piece = total[j * size : (j + 1) * size]
            self.zw[j] = piece
            self.zs[j] = piece.astype(BF)
        loop(1, self.n, lambda k: self.scatter(k, False).start())

    def send_totals(self):
        def add(k, total):
            self.scatter(k, True).wait_recv()
            return total + self.zr[lax.rem(self.me + k, self.n)].astype(F32)

        total = lax.fori_loop(1, self.n, add, self.zw[self.me])
        self.res[self.r, self.odd, self.me] = total.astype(BF)
        loop(1, self.n, lambda k: self.gather(k, False).start())

    def send_back(self):
        loop(1, self.n, lambda k: self.gather(k, True).wait_recv())
        self.cross_back().start()
        self.pair_back(0).start()

    def send_other(self):
        self.cross_back().wait_recv()
        self.pair_back(1).start()

    def finish(self):
        self.pair_back(0).wait()
        self.pair_back(1).wait()
        self.cross_back().wait_send()

        def sent(k):
            self.scatter(k, False).wait_send()
            self.gather(k, False).wait_send()

        loop(1, self.n, sent)

def codec_kernel(
    frames, refs_ref, window_ref, level_ref, *rest,
):
    inputs, rest = rest[:7], rest[7:]
    (coded_hbm, lat_hbm), totals, rest = rest[:2], rest[2 : 2 + 2 * LANES], rest[2 + 2 * LANES :]
    held, rest = rest[:9], rest[9:]
    x_ref, ct_ref, qs_ref, sp_ref, vp_ref, op_ref, taps_ref, coded_ref, lat_ref = held
    chunks = x_ref.shape[0] // (WMAX * COLS)
    buf_refs, rest = rest[:chunks], rest[chunks:]
    (
        halo_ref, q_ref, do_ref, gp_ref, resid_ref, cth_ref, ext_ref, xi_ref, k_ref,
        v_ref, kt_ref, vt_ref, mix_ref, dq_ref, dk_ref, dv_ref, p_ref, pb_ref, inv_ref, dp_ref,
        ds_ref, qm_ref, dom_ref, residual_ref, hx_ref, eh_ref, ph_ref, pg_ref, edge_ref, out_ref, rb_ref,
        sb_ref, ssem, rsem, hs, hr, bs, br, one, local_sems,
    ), sums = rest[:40], rest[40:]
    f = lax.axis_index("frame")
    r = lax.axis_index("row")
    tokens, width = x_ref.shape
    rows = tokens // COLS
    rim = WMAX * COLS
    step = rim

    def row_at(i):
        return pl.multiple_of(jnp.where(r == 0, i, rows - 1 - i) * COLS, COLS)

    odd = lax.rem(f, 2)
    pair = f + 1 - 2 * odd
    lo2, hi2, lo4, hi4 = f >= 2, f + 2 < frames, f >= 4, f + 4 < frames
    side = ((odd == 1) & (f + 1 < frames)) | ((odd == 0) & (f >= 1))
    relay = ((odd == 1) & lo2) | ((odd == 0) & hi2)
    always = f >= 0
    partner = {"row": 1 - r}
    up, down, across = {"frame": f + 2}, {"frame": f - 2}, {"frame": pair}
    lanes = [
        Sum(sums[12 * i : 12 * i + 12], totals[i], f, r, frames) for i in range(2 * LANES)
    ]
    weights, projections = lanes[:LANES], lanes[LANES:]

    loads = [
        pltpu.make_async_copy(source, target, local_sems.at[i])
        for i, (source, target) in enumerate(zip(inputs, held))
    ]
    for load in loads:
        load.start()
    barrier = pltpu.get_barrier_semaphore()
    pl.semaphore_signal(barrier, inc=1, device_id=partner, device_id_type=MESH)
    pl.semaphore_signal(barrier, inc=1, device_id=across, device_id_type=MESH)

    def hello(k):
        other = {"frame": lax.rem(f + 2 * k, frames)}
        pl.semaphore_signal(barrier, inc=1, device_id=other, device_id_type=MESH)

    loop(1, frames // 2, hello)
    pl.semaphore_wait(barrier, frames // 2 + 1)

    def link(i, source, target, device):
        return pltpu.make_async_remote_copy(
            source, target, one.at[2 * i], one.at[2 * i + 1],
            device_id=device, device_id_type=MESH,
        )

    def place(c):
        return pl.multiple_of(jnp.where(r == 0, chunks - 1 - c, c) * step, step)

    loads[0].wait()
    edge = pl.multiple_of((1 - r) * (tokens - COLS), COLS)

    def copy(kind, c, source, device):
        if source is x_ref:
            source = x_ref.at[pl.ds(place(c), step)]
        return pltpu.make_async_remote_copy(
            source, buf_refs[c].at[kind], ssem.at[kind, c], rsem.at[kind, c],
            device_id=device, device_id_type=MESH,
        )

    def halo(kind):
        return pltpu.make_async_remote_copy(
            buf_refs[0].at[kind], halo_ref.at[kind], hs.at[kind], hr.at[kind],
            device_id=partner, device_id_type=MESH,
        )

    have = (lo2, hi2, always, lo4, hi4, side)
    hops = ((0, hi2, up), (1, lo2, down), (2, always, across))

    def launch(c):
        for kind, exists, target in hops:

            @pl.when(exists)
            def _():
                copy(kind, c, x_ref, target).start()

    def launched(c):
        for kind, exists, target in hops:

            @pl.when(exists)
            def _():
                copy(kind, c, x_ref, target).wait_send()

    launch(0)
    launch(1)
    for load in loads[1:]:
        load.wait()
    ct_copy = link(0, ct_ref.at[pl.ds(edge, COLS)], cth_ref, partner)
    ct_copy.start()

    def pass_on(c):
        @pl.when(lo2)
        def _():
            copy(0, c, x_ref, across).wait_recv()
            if c == 0:
                halo(0).start()

        @pl.when(lo2 & hi2)
        def _():
            copy(3, c, buf_refs[c].at[0], up).start()

        @pl.when(lo2 & (odd == 1))
        def _():
            copy(5, c, buf_refs[c].at[0], across).start()

        @pl.when(hi2)
        def _():
            copy(1, c, x_ref, across).wait_recv()
            if c == 0:
                halo(1).start()

        @pl.when(hi2 & lo2)
        def _():
            copy(4, c, buf_refs[c].at[1], down).start()

        @pl.when(hi2 & (odd == 0))
        def _():
            copy(5, c, buf_refs[c].at[1], across).start()

    level = lax.broadcasted_iota(jnp.int32, (qs_ref.shape[0], 1), 0)
    gain = jnp.sum(
        jnp.where(level == level_ref[0], qs_ref[...], 0.0), axis=0, keepdims=True
    )
    q_ref[...] = mm(x_ref[...], sp_ref[...]).astype(BF)
    grad_z = ct_ref[...].astype(F32) * gain
    resid_ref[...] = grad_z
    grad_zb = grad_z.astype(BF)
    gp_ref[: 2 * COLS, :] = jnp.zeros((2 * COLS, width), BF)
    gp_ref[2 * COLS : 2 * COLS + tokens, :] = grad_zb
    gp_ref[2 * COLS + tokens :, :] = jnp.zeros((2 * COLS, width), BF)
    ext_ref[COLS : COLS + tokens, :] = grad_zb
    dk_ref[...] = jnp.zeros_like(dk_ref)
    dv_ref[...] = jnp.zeros_like(dv_ref)
    got = (lo2, hi2, always, lo2 & hi2, lo2 & hi2, relay)
    for kind in (0, 1, 3, 4, 5):

        @pl.when(jnp.logical_not(got[kind]))
        def _():
            rb_ref[kind, :, :] = jnp.zeros((tokens, width), BF)

    launched(0)
    launch(2)
    ct_copy.wait()
    outer = (cth_ref[...].astype(F32) * gain).astype(BF)
    blank = jnp.zeros_like(outer)
    ext_ref[:COLS, :] = jnp.where(r == 0, blank, outer)
    ext_ref[COLS + tokens :, :] = jnp.where(r == 0, outer, blank)
    pass_on(0)
    for c in range(3, chunks):
        launched(c - 2)
        launch(c)
    resid = resid_ref[...]
    for t in range(3):
        resid = resid + mm(ext_ref[(2 - t) * COLS : (2 - t) * COLS + tokens, :], taps_ref[t], 1, 1)
    resid_ref[...] = resid
    pass_on(1)
    do_ref[...] = mm(resid_ref[...].astype(BF), op_ref[...], 1, 1).astype(BF)
    copy(2, 0, x_ref, across).wait_recv()
    halo(2).start()
    for c in range(max(0, chunks - 2), chunks):
        launched(c)
    for c in range(2, chunks):
        pass_on(c)
    for i in range(rows):
        tok = pl.ds(row_at(i), COLS)
        query, grad = q_ref[tok, :], do_ref[tok, :]
        for hf in range(2):
            qm_ref[i, hf] = masked_rows(query, hf * HALF * DH)
            dom_ref[i, hf] = masked_rows(grad, hf * HALF * DH)
    sources = (f - 2, f + 2, pair, f - 4, f + 4, f - 1 + 2 * odd)
    targets = (f + 2, f - 2, pair, f + 4, f - 4, f - 1 + 2 * odd)
    kinds = []
    for s in range(2):
        own = refs_ref[0, s]
        kind = jnp.int32(0)
        for number, source in enumerate(sources):
            kind = jnp.where(own == source, number, kind)
        kinds.append(kind)

    def arrive(c):
        for kind in range(2, KINDS):
            if kind > 2 or c:

                @pl.when(have[kind])
                def _():
                    copy(kind, c, x_ref, across).wait_recv()
                    if c == 0:
                        halo(kind).start()

    def take(first, piece):
        for d in range(WMAX):
            for s in range(2):
                at = (2 * (first + d) + s) * COLS
                xi_ref[at : at + COLS, :] = piece(s, d)
        part = slice(2 * first * COLS, 2 * (first + WMAX) * COLS)
        keys = mm(xi_ref[part, :], sp_ref[...]).astype(BF)
        k_ref[part, :] = keys
        kt_ref[:, part] = keys.T
        vals = mm(xi_ref[part, :], vp_ref[...]).astype(BF)
        v_ref[part, :] = vals
        vt_ref[:, part] = vals.T

    def sub(d):
        return pl.ds(pl.multiple_of(jnp.where(r == 0, d, 1 - d) * COLS, COLS), COLS)

    def take_chunk(c):
        take(WMAX + rows - WMAX * (c + 1), lambda s, d: buf_refs[c][kinds[s], sub(d), :])

    window = window_ref[0]
    bias = [
        jnp.where(abs(c - WMAX) <= window, 0.0, -jnp.inf).astype(F32) for c in range(2 * WMAX + 1)
    ]

    def forward(last, first):
        for i in range(last, first - 1, -1):
            forward_row(i, bias, k_ref, qm_ref, p_ref, pb_ref, inv_ref)

    def mix(last, first):
        for i in range(last, first - 1, -1):
            mix_row(i, row_at(i), vt_ref, pb_ref, mix_ref)

    def project(first):
        part = slice(2 * first * COLS, 2 * (first + WMAX) * COLS)
        return mm(dk_ref[part, :].astype(BF), sp_ref[...], 1, 1) + mm(
            dv_ref[part, :].astype(BF), vp_ref[...], 1, 1
        )

    part_copy = link(2, ph_ref, pg_ref, partner)
    sent = (hi2, lo2, always, hi4, lo4, side)
    device = (up, down, across, up, down, across)

    def give(kind, c, source):
        part = pl.ds(place(c), step)
        return pltpu.make_async_remote_copy(
            source.at[part], rb_ref.at[kind, part], bs.at[kind, c], br.at[kind, c],
            device_id=device[kind], device_id_type=MESH,
        )

    def hand_out(c):
        first = rows - WMAX * (c + 1)
        block = project(WMAX + first)
        if c == 0:
            band = 2 * COLS
            block = block + jnp.concatenate([pg_ref[band:, :], pg_ref[:band, :]], axis=0).astype(F32)
        for kind, target in enumerate(targets):
            one_is = refs_ref[0, 0] == target
            two_is = refs_ref[0, 1] == target
            for d in range(WMAX):
                part = jnp.where(one_is, block[2 * d * COLS : (2 * d + 1) * COLS], 0.0)
                part = part + jnp.where(two_is, block[(2 * d + 1) * COLS : (2 * d + 2) * COLS], 0.0)
                out_ref[kind, pl.ds(row_at(first + d), COLS), :] = part.astype(BF)
        for kind in (3, 4, 5):

            @pl.when(sent[kind])
            def _():
                give(kind, c, out_ref.at[kind]).start()

    even = jnp.where(odd == 0, 1.0, 0.0).astype(F32)

    def merge(c):
        for kind in (3, 4, 5):

            @pl.when(got[kind])
            def _():
                give(kind, c, out_ref.at[kind]).wait_recv()

        give(2, c, out_ref.at[2]).start()
        part = pl.ds(place(c), step)
        extra = rb_ref[5, part, :].astype(F32)
        rising = out_ref[0, part, :].astype(F32) + rb_ref[3, part, :].astype(F32) + extra * even
        falling = (
            out_ref[1, part, :].astype(F32) + rb_ref[4, part, :].astype(F32) + extra * (1.0 - even)
        )
        sb_ref[0, part, :] = rising.astype(BF)
        sb_ref[1, part, :] = falling.astype(BF)

        @pl.when(hi2)
        def _():
            give(0, c, sb_ref.at[0]).start()

        @pl.when(lo2)
        def _():
            give(1, c, sb_ref.at[1]).start()

    def collect(c):
        for kind in (0, 1, 2):

            @pl.when(got[kind])
            def _():
                give(kind, c, out_ref.at[kind]).wait_recv()

        part = pl.ds(place(c), step)
        lat_ref[part, :] = (
            resid_ref[part, :]
            + rb_ref[0, part, :].astype(F32)
            + rb_ref[1, part, :].astype(F32)
            + rb_ref[2, part, :].astype(F32)
        ).astype(BF)

    def finish_forward():
        residual = x_ref[...].astype(F32) + mm(mix_ref[...], op_ref[...])
        residual_ref[...] = residual
        hx_ref[COLS : COLS + tokens, :] = residual.astype(BF)

        def fill(half, side, value):
            size = width // LANES
            for i, lane in enumerate(weights):
                lane.w[half, side] = value[i * size : (i + 1) * size]

        fill(0, 0, mm(mix_ref[...].T, resid_ref[...].astype(BF)))
        hidden_copy.wait()
        outer = eh_ref[...]
        blank = jnp.zeros_like(outer)
        hx_ref[:COLS, :] = jnp.where(r == 0, blank, outer)
        hx_ref[COLS + tokens :, :] = jnp.where(r == 0, outer, blank)
        hxt = hx_ref[...].T
        span = tokens + 2 * COLS
        for t in range(3):
            fill((t + 1) // 2, (t + 1) % 2, mm(hxt, gp_ref[(2 - t) * COLS : (2 - t) * COLS + span, :]))
        for lane in weights:
            lane.begin()

    def back(last, first):
        for i in range(last, first - 1, -1):
            score_row(i, v_ref, dom_ref, p_ref, inv_ref, dp_ref, ds_ref)
        for i in range(last, first - 1, -1):
            key_row(i, qm_ref, dom_ref, pb_ref, ds_ref, dk_ref, dv_ref)
            query_row(i, row_at(i), kt_ref, ds_ref, dq_ref)

    arrive(0)
    arrive(1)
    take_chunk(0)
    take_chunk(1)
    for kind in range(KINDS):

        @pl.when(have[kind])
        def _():
            halo(kind).wait()

    take(WMAX + rows, lambda s, d: halo_ref[kinds[s], sub(d), :])
    low = rows - WMAX
    forward(rows - 1, low)
    mix(rows - 1, low)
    inner = row_at(rows - 1)
    edge_ref[...] = (
        x_ref[pl.ds(inner, COLS), :].astype(F32) + mm(mix_ref[pl.ds(inner, COLS), :], op_ref[...])
    ).astype(BF)
    hidden_copy = link(1, edge_ref, eh_ref, partner)
    hidden_copy.start()
    back(rows - 1, low)
    ph_ref[...] = project(WMAX + rows).astype(BF)
    part_copy.start()
    for c in range(2, chunks):
        arrive(c)
        take_chunk(c)
        below = low - WMAX if c < chunks - 1 else 0
        forward(low - 1, below)
        mix(low - 1, below)
        if c == chunks - 1:
            finish_forward()
        for top in range(low, below, -WMAX):
            back(top - 1, top - WMAX)
            done = (rows - top) // WMAX - 1
            if done == 0:
                part_copy.wait()
            if done < chunks - WMAX:
                hand_out(done)
            if c == chunks - 1 and done == 1:
                for lane in weights:
                    lane.send_cross()
        low = below
    inside = 2 * WMAX * COLS
    xit = xi_ref[inside:, :].T
    grad_shared = mm(x_ref[...].T, dq_ref[...]) + mm(xit, dk_ref[inside:, :].astype(BF))
    grad_values = mm(xit, dv_ref[inside:, :].astype(BF))
    short = width // (2 * LANES)
    for i, lane in enumerate(projections):
        for side_ in range(2):
            part = slice((2 * i + side_) * short, (2 * i + side_ + 1) * short)
            lane.w[0, side_] = grad_shared[part]
            lane.w[1, side_] = grad_values[part]
        lane.begin()
    hand_out(chunks - 2)
    hand_out(chunks - 1)
    for lane in projections:
        lane.send_cross()
    for lane in weights:
        lane.send_pieces()
    merge(0)
    for lane in projections:
        lane.send_pieces()
    merge(1)
    for lane in weights:
        lane.send_totals()
    for lane in projections:
        lane.send_totals()
    merge(2)
    merge(3)
    resid_ref[...] = resid_ref[...] + mm(dq_ref[...], sp_ref[...], 1, 1)
    context = residual_ref[...]
    for t in range(3):
        context = context + mm(hx_ref[t * COLS : t * COLS + tokens, :], taps_ref[t])
    coded_ref[...] = (context * gain).astype(BF)
    coded_save = pltpu.make_async_copy(coded_ref, coded_hbm, local_sems.at[7])
    coded_save.start()
    for lane in weights:
        lane.send_back()
    for lane in projections:
        lane.send_back()
    collect(0)
    for lane in weights:
        lane.send_other()
    for lane in projections:
        lane.send_other()
    for c in range(1, chunks):
        collect(c)
    lat_save = pltpu.make_async_copy(lat_ref, lat_hbm, local_sems.at[8])
    lat_save.start()
    for lane in lanes:
        lane.finish()

    for kind in range(KINDS):

        if kind > 2:

            @pl.when(got[kind])
            def _():
                for c in range(chunks):
                    copy(kind, c, x_ref, across).wait_send()

        @pl.when(sent[kind])
        def _():
            for c in range(chunks):
                give(kind, c, out_ref.at[kind]).wait_send()

    coded_save.wait()
    lat_save.wait()


def sum_scratch(size, width, n):
    dma = pltpu.SemaphoreType.DMA
    return [
        pltpu.VMEM((2, 2, size, width), F32),
        pltpu.VMEM((2, size, width), F32),
        pltpu.VMEM((size, width), BF),
        pltpu.VMEM((size, width), BF),
        pltpu.VMEM((n, size // n, width), F32),
        pltpu.VMEM((n, size // n, width), BF),
        pltpu.VMEM((n, size // n, width), BF),
        dma((10,)), dma((n,)), dma((n,)), dma((n,)), dma((n,)),
    ]


def scale_kernel(norm, coded_ref, lat_ref, *rest):
    totals = rest[: 2 * LANES]
    coded_out, lat_out, gs_ref, gv_ref, go_ref, gt_ref = rest[2 * LANES :]
    coded_out[...] = coded_ref[...]
    lat_out[...] = lat_ref[...]
    for i in range(LANES):
        large, small = totals[i], totals[LANES + i]
        pieces, size = large.shape[2:4]
        short = small.shape[3]
        for j in range(pieces):
            at = pl.ds((i * pieces + j) * size, size)
            go_ref[at, :] = large[0, 0, j].astype(F32) * norm
            for t in range(3):
                gt_ref[t, at, :] = large[(t + 1) // 2, (t + 1) % 2, j].astype(F32) * norm
            for side in range(2):
                at = pl.ds(((2 * i + side) * pieces + j) * short, short)
                gs_ref[at, :] = small[0, side, j].astype(F32) * norm
                gv_ref[at, :] = small[1, side, j].astype(F32) * norm


def local(
    latents, ref_frames, windows, quant_level, quant_scale,
    shared_proj, value_proj, output_proj, conv_taps, cotangent,
):
    tokens, width = latents.shape[1:]
    frames = lax.axis_size("frame")
    rows = tokens // COLS
    ext = tokens + 2 * WMAX * COLS
    keys = 2 * (2 * WMAX + 1) * COLS
    wide = HALF * COLS
    rim = WMAX * COLS
    chunks = tokens // rim
    vm = pl.BlockSpec(memory_space=pltpu.VMEM)
    sm = pl.BlockSpec(memory_space=pltpu.SMEM)
    hbm = pl.BlockSpec(memory_space=pltpu.MemorySpace.HBM)
    dma = pltpu.SemaphoreType.DMA
    slab = jax.ShapeDtypeStruct((tokens, width), BF)
    square = jax.ShapeDtypeStruct((width, width), F32)
    pairs = frames // 2
    sizes = (width // LANES,) * LANES + (width // (2 * LANES),) * LANES

    def rows_of(count, kind=BF):
        return pltpu.VMEM((count, width), kind)

    coded, grad_latents, *totals = pl.pallas_call(
        functools.partial(codec_kernel, frames),
        out_shape=(
            slab, slab,
        )
        + tuple(
            jax.ShapeDtypeStruct((2, 2, pairs, size // pairs, width), BF) for size in sizes
        ),
        in_specs=[sm] * 3 + [hbm] * 7,
        out_specs=(hbm, hbm) + (vm,) * (2 * LANES),
        scratch_shapes=[
            rows_of(tokens), rows_of(tokens), pltpu.VMEM(quant_scale.shape, F32),
            rows_of(width), rows_of(width), rows_of(width),
            pltpu.VMEM(conv_taps.shape, BF), rows_of(tokens), rows_of(tokens),
        ]
        + [pltpu.VMEM((KINDS, rim, width), BF)] * (chunks + 1)
        + [
            rows_of(tokens), rows_of(tokens), rows_of(tokens + 4 * COLS), rows_of(tokens, F32),
            rows_of(COLS), rows_of(tokens + 2 * COLS),
            rows_of(2 * ext), rows_of(2 * ext), rows_of(2 * ext),
            pltpu.VMEM((width, 2 * ext), BF),
            pltpu.VMEM((width, 2 * ext), BF),
            rows_of(tokens), rows_of(tokens), rows_of(2 * ext, F32), rows_of(2 * ext, F32),
            pltpu.VMEM((rows, 2, keys, wide), F32),
            pltpu.VMEM((rows, 2, keys, wide), BF),
            pltpu.VMEM((rows, 2, 1, wide), F32),
            pltpu.VMEM((RING, 2, keys, wide), F32),
            pltpu.VMEM((RING, 2, keys, wide), BF),
            pltpu.VMEM((rows, 2, wide, HALF * DH), BF),
            pltpu.VMEM((rows, 2, wide, HALF * DH), BF),
            rows_of(tokens, F32), rows_of(tokens + 2 * COLS), rows_of(COLS),
            rows_of(2 * rim), rows_of(2 * rim), rows_of(COLS),
            pltpu.VMEM((KINDS, tokens, width), BF),
            pltpu.VMEM((KINDS, tokens, width), BF),
            pltpu.VMEM((2, tokens, width), BF),
            dma((KINDS, chunks)), dma((KINDS, chunks)), dma((KINDS,)), dma((KINDS,)),
            dma((KINDS, chunks)), dma((KINDS, chunks)), dma((6,)), dma((9,)),
        ]
        + [ref for size in sizes for ref in sum_scratch(size, width, pairs)],
        compiler_params=pltpu.CompilerParams(
            collective_id=0, has_side_effects=True, vmem_limit_bytes=64_000_000
        ),
        name="codec",
    )(
        ref_frames, windows, quant_level, latents[0], cotangent[0], quant_scale,
        shared_proj, value_proj, output_proj, conv_taps,
    )
    total = frames * lax.axis_size("row") * tokens
    coded, grad_latents, grad_shared, grad_values, grad_output, grad_taps = pl.pallas_call(
        functools.partial(scale_kernel, 1.0 / math.sqrt(total)),
        out_shape=(
            slab, slab, square, square, square, jax.ShapeDtypeStruct((3, width, width), F32),
        ),
        in_specs=[vm] * (2 + 2 * LANES),
        out_specs=(vm,) * 6,
        name="scale",
    )(coded, grad_latents, *totals)
    return (
        coded[None], grad_latents[None], grad_shared, grad_values, grad_output, grad_taps
    )


def solution(mesh):
    tok = P(("groups", "frame"), "row", None)
    frm = P(("groups", "frame"))
    placed = (tok, P(("groups", "frame"), None), frm, frm, P(), P(), P(), P(), P(), tok)
    return jax.shard_map(
        local,
        mesh=mesh,
        in_specs=placed,
        out_specs=(
            tok, tok, P("groups", None), P("groups", None), P("groups", None),
            P("groups", None, None),
        ),
        check_vma=False,
    )
```
